1024 devices in a mesh: grp: 4 (over x_lo), gx: 8 (over z), gy: 32 (over x_hi, y, core).
Axes of the slice: x: 8 (x_hi: 2, x_lo: 4; x = x_hi * 4 + x_lo), y: 8, z: 8, core: 2. Of those that a mesh axis runs over, the one named last changes fastest.
Arguments:
- zonal_boundary_speed: float32 [32, 32, 4, 1024], P(None, 'gy', 'grp', 'gx'), may hold values from -0.2 to 0.2
- meridional_boundary_speed: float32 [32, 32, 4, 1024], P(None, 'gy', 'grp', 'gx'), may hold values from -0.2 to 0.2
- potential_warmth: float32 [32, 32, 4, 1024], P(None, 'gy', 'grp', 'gx'), may hold values from 2 to 28
- saltiness_field: float32 [32, 32, 4, 1024], P(None, 'gy', 'grp', 'gx'), may hold values from 33 to 37
- quiescent_mixing_profile: float32 [32, 32, 4, 1024], P(None, 'gy', 'grp', 'gx'), may hold values from 0.005 to 0.05
- substance_amounts: float32 [19, 32, 128, 1024], P(None, 'grp', 'gy', 'gx'), may hold values from 0.1 to 3
- submerged_layer_number: int32 [128, 1024], P('gy', 'gx'), may hold values from 0 to 32
- solar_radiation: float32 [128, 1024], P('gy', 'gx'), may hold values from 0.2 to 1
- interaction_rates: float32 [19, 19], replicated, may hold values from -1.25 to 1.25
- photosynthetic_rates: float32 [19], replicated, may hold values from 0.1 to 1
- saturation_irradiance: float32 [19], replicated, may hold values from 0.05 to 0.5
- pigment_per_tracer: float32 [19], replicated, may hold values from 0.01 to 0.1
Outputs:
- east_final: float32 [32, 32, 4, 1024], P(None, 'gy', 'grp', 'gx')
- north_final: float32 [32, 32, 4, 1024], P(None, 'gy', 'grp', 'gx')
- temperature_final: float32 [32, 32, 4, 1024], P(None, 'gy', 'grp', 'gx')
- salinity_final: float32 [32, 32, 4, 1024], P(None, 'gy', 'grp', 'gx')
- tracers_final: float32 [19, 32, 128, 1024], P(None, 'grp', 'gy', 'gx')
The draws below stay inside these ranges and needn't reach their ends.
All inputs are finite; a program needn't handle non-finite values.
Results may differ from the reference program's by a relative error of at most 0.0001.
Values sent between devices are 32-bit elements; how exact they have to be, the bound alone decides.
A program may use at most 32 MiB of HBM per device.

```python
import math
import jax
import jax.numpy as jnp
from jax import lax

NTR = 19
DEPTH_LAYERS = 32
PIECE_LATITUDES = 4
STEPS = 2
MESH_WIDTH = 1024
NY = 128
MERIDIAN_PIECES = 32


def plant(values, key, low, high):
    longest = values.shape.index(max(values.shape))
    spots = []
    for shift in (0, 1):
        where = [jax.random.randint(jax.random.fold_in(key, axis), (), 0, length) for axis, length in enumerate(values.shape)]
        where[longest] = (where[longest] + shift) % values.shape[longest]
        spots.append(tuple(where))
    return values.at[spots[0]].set(low).at[spots[1]].set(high)


def shard_levels(key, extent, split, least, largest):
    def one(axis_at, parts):
        steps = jax.random.uniform(jax.random.fold_in(jax.random.fold_in(key, 6), axis_at), (parts,), jnp.float32, least / len(split), largest / len(split))
        return jnp.repeat(jnp.exp(steps), extent[axis_at] // parts).reshape((-1,) + (1,) * (len(extent) - axis_at - 1))

    level = one(*split[0])
    for cut in split[1:]:
        level = level * one(*cut)
    return level


def gaussian(stream_key, dims, width, limit, dtype=jnp.bfloat16):
    result = width * jax.random.normal(stream_key, dims, jnp.float32)
    return jnp.clip(result, min=-limit, max=limit).astype(dtype)


def setup_inputs(seed: int = 0) -> dict:
    keys = jax.random.split(jax.random.key(seed), 13)
    return {
        "zonal_boundary_speed": jnp.clip(jax.random.uniform(keys[0], (DEPTH_LAYERS, MERIDIAN_PIECES, PIECE_LATITUDES, MESH_WIDTH), jnp.float32, -0.2, 0.2) * shard_levels(keys[0], (DEPTH_LAYERS, MERIDIAN_PIECES, PIECE_LATITUDES, MESH_WIDTH), ((1, 32), (2, 4), (3, 8)), -0.4, 0.0), -0.2, 0.2),
        "meridional_boundary_speed": jnp.clip(jax.random.uniform(keys[1], (DEPTH_LAYERS, MERIDIAN_PIECES, PIECE_LATITUDES, MESH_WIDTH), jnp.float32, -0.2, 0.2) * shard_levels(keys[1], (DEPTH_LAYERS, MERIDIAN_PIECES, PIECE_LATITUDES, MESH_WIDTH), ((1, 32), (2, 4), (3, 8)), -0.4, 0.0), -0.2, 0.2),
        "potential_warmth": jnp.clip(2.0 + 26.0 * jax.random.uniform(keys[2], (DEPTH_LAYERS, MERIDIAN_PIECES, PIECE_LATITUDES, MESH_WIDTH), jnp.float32) ** shard_levels(keys[2], (DEPTH_LAYERS, MERIDIAN_PIECES, PIECE_LATITUDES, MESH_WIDTH), ((1, 32), (2, 4), (3, 8)), -0.2, 0.2), 2.0, 28.0),
        "saltiness_field": jnp.clip(33.0 + 4.0 * jax.random.uniform(keys[3], (DEPTH_LAYERS, MERIDIAN_PIECES, PIECE_LATITUDES, MESH_WIDTH), jnp.float32) ** shard_levels(keys[3], (DEPTH_LAYERS, MERIDIAN_PIECES, PIECE_LATITUDES, MESH_WIDTH), ((1, 32), (2, 4), (3, 8)), -0.2, 0.2), 33.0, 37.0),
        "quiescent_mixing_profile": jnp.clip(jnp.exp(math.log(0.05) - 2.3025851 * jax.random.uniform(keys[4], (DEPTH_LAYERS, MERIDIAN_PIECES, PIECE_LATITUDES, MESH_WIDTH), jnp.float32) ** shard_levels(keys[4], (DEPTH_LAYERS, MERIDIAN_PIECES, PIECE_LATITUDES, MESH_WIDTH), ((1, 32), (2, 4), (3, 8)), -0.2, 0.2)), 0.005, 0.05),
        "substance_amounts": jnp.clip(jnp.exp(math.log(3.0) - 3.4011974 * jax.random.uniform(keys[5], (NTR, DEPTH_LAYERS, NY, MESH_WIDTH), jnp.float32) ** shard_levels(keys[5], (NTR, DEPTH_LAYERS, NY, MESH_WIDTH), ((1, 4), (2, 32), (3, 8)), -0.2, 0.2)), 0.1, 3.0),
        "submerged_layer_number": plant(jax.random.randint(keys[6], (NY, MESH_WIDTH), 0, DEPTH_LAYERS + 1), jax.random.fold_in(keys[6], 1), 0, DEPTH_LAYERS).astype(jnp.int32),
        "solar_radiation": jnp.clip(jnp.exp(math.log(1.0) - 1.609438 * jax.random.uniform(keys[7], (NY, MESH_WIDTH), jnp.float32) ** shard_levels(keys[7], (NY, MESH_WIDTH), ((0, 32), (1, 8)), -0.2, 0.2)), 0.2, 1.0),
        "interaction_rates": gaussian(keys[8], (NTR, NTR), NTR ** -0.5, 1.25, jnp.float32),
        "photosynthetic_rates": jnp.clip(jnp.exp(jax.random.uniform(keys[9], (NTR,), jnp.float32, math.log(0.1), math.log(1.0))), 0.1, 1.0),
        "saturation_irradiance": jnp.clip(jnp.exp(jax.random.uniform(keys[10], (NTR,), jnp.float32, math.log(0.05), math.log(0.5))), 0.05, 0.5),
        "pigment_per_tracer": jnp.clip(jnp.exp(jax.random.uniform(keys[11], (NTR,), jnp.float32, math.log(0.01), math.log(0.1))), 0.01, 0.1),
    }


WATER_ATTEN = 0.01
PIGMENT_ATTEN = 0.05
WARMING_UPTAKE = 5.0
WARM_EXPANSION = 0.2
SALT_EXPANSION = 0.8
CONVECT_MIX = 0.15
SIDE_DIFFUSE = 0.05
WARMING_FACTOR = 0.0633
TIME_STEP = 0.5


def trim_axis(values, dimension_slot, start, stop):
    leading = (slice(None),) * (values.ndim + dimension_slot)
    return values[leading + (slice(start, stop),)]


def pad_axis(values, dimension_slot):
    widths = [(0, 0)] * values.ndim
    widths[dimension_slot] = (1, 1)
    return jnp.pad(values, widths)


def face_divergence(tracer_amounts, velocity, submerged_mask, dimension_slot):
    lower_conc = trim_axis(tracer_amounts, dimension_slot, None, -1)
    upper_conc = trim_axis(tracer_amounts, dimension_slot, 1, None)
    face_speed = trim_axis(velocity, dimension_slot, None, -1)
    opening = trim_axis(submerged_mask, dimension_slot, None, -1) * trim_axis(submerged_mask, dimension_slot, 1, None)
    flux_face = opening * (jnp.maximum(face_speed, 0.0) * lower_conc + jnp.minimum(face_speed, 0.0) * upper_conc - SIDE_DIFFUSE * (upper_conc - lower_conc))
    return trim_axis(flux_face, dimension_slot, 1, None) - trim_axis(flux_face, dimension_slot, None, -1)


def level_divergence(tracer_amounts, mixing_coefficient):
    flux_face = trim_axis(mixing_coefficient, -3, None, -1) * (trim_axis(tracer_amounts, -3, 1, None) - trim_axis(tracer_amounts, -3, None, -1))
    return trim_axis(flux_face, -3, 1, None) - trim_axis(flux_face, -3, None, -1)


def light_columns(pigment, surface):
    attenuation = WATER_ATTEN + PIGMENT_ATTEN * pigment
    above = jnp.cumsum(attenuation, axis=0) - attenuation
    top_light = surface * jnp.exp(-above)
    return top_light * (1.0 - jnp.exp(-attenuation)), top_light * jnp.exp(-0.5 * attenuation)


def marine_advance(zonal_transport, meridional_transport, thermal_mesh, brine_values, quiescent_mixing, radiative_warming, submerged_mask):
    thermal_mesh = thermal_mesh + WARMING_UPTAKE * radiative_warming * submerged_mask
    water_buoyancy = SALT_EXPANSION * brine_values - WARM_EXPANSION * thermal_mesh
    strat = water_buoyancy[1:] - water_buoyancy[:-1]
    face_mix = (0.5 * (quiescent_mixing[:-1] + quiescent_mixing[1:]) + CONVECT_MIX * jax.nn.sigmoid(-strat)) * submerged_mask[1:]
    bottom = jnp.zeros_like(face_mix[:1])
    mixing_coefficient = jnp.concatenate([face_mix, bottom], axis=0)

    def turbulent_stirring(field):
        flux_face = face_mix * (field[1:] - field[:-1])
        return field + jnp.concatenate([flux_face, bottom], axis=0) - jnp.concatenate([bottom, flux_face], axis=0)

    return turbulent_stirring(zonal_transport), turbulent_stirring(meridional_transport), turbulent_stirring(thermal_mesh), turbulent_stirring(brine_values), mixing_coefficient


def chemical_kinetics(tracer_amounts, thermal_mesh, photosynthetic_radiance, submerged_mask, interaction_rates, photosynthetic_rates, saturation_irradiance):
    thermal_multiplier = jnp.exp(WARMING_FACTOR * (thermal_mesh - 20.0))
    mixed_terms = jnp.einsum("ij,jzyx->izyx", interaction_rates, tracer_amounts, precision=lax.Precision.HIGHEST)
    light_limit = photosynthetic_radiance / (photosynthetic_radiance + saturation_irradiance[:, None, None, None])
    return TIME_STEP * submerged_mask * (thermal_multiplier * mixed_terms + photosynthetic_rates[:, None, None, None] * light_limit * tracer_amounts)


def reference(zonal_boundary_speed, meridional_boundary_speed, potential_warmth, saltiness_field, quiescent_mixing_profile, substance_amounts, submerged_layer_number, solar_radiation, interaction_rates, photosynthetic_rates, saturation_irradiance, pigment_per_tracer):
    mesh_shape_sizes = (DEPTH_LAYERS, NY, MESH_WIDTH)
    zonal_transport = zonal_boundary_speed.reshape(mesh_shape_sizes)
    meridional_transport = meridional_boundary_speed.reshape(mesh_shape_sizes)
    thermal_mesh = potential_warmth.reshape(mesh_shape_sizes)
    brine_values = saltiness_field.reshape(mesh_shape_sizes)
    quiescent_mixing = quiescent_mixing_profile.reshape(mesh_shape_sizes)
    submerged_mask = (lax.broadcasted_iota(jnp.int32, mesh_shape_sizes, 0) < submerged_layer_number[None]).astype(jnp.float32)
    tracer_amounts = substance_amounts
    for repeat in range(STEPS):
        pigment = jnp.einsum("i,izyx->zyx", pigment_per_tracer, tracer_amounts, precision=lax.Precision.HIGHEST)
        radiative_warming, photosynthetic_radiance = light_columns(pigment, solar_radiation[None])
        zonal_transport, meridional_transport, thermal_mesh, brine_values, mixing_coefficient = marine_advance(zonal_transport, meridional_transport, thermal_mesh, brine_values, quiescent_mixing, radiative_warming, submerged_mask)
        zonal_increment = face_divergence(pad_axis(tracer_amounts, -1), pad_axis(zonal_transport, -1), pad_axis(submerged_mask, -1), -1)
        meridional_increment = face_divergence(pad_axis(tracer_amounts, -2), pad_axis(meridional_transport, -2), pad_axis(submerged_mask, -2), -2)
        depthwise_transfer = level_divergence(pad_axis(tracer_amounts, -3), pad_axis(mixing_coefficient, -3))
        tracer_amounts = tracer_amounts - zonal_increment - meridional_increment + depthwise_transfer + chemical_kinetics(tracer_amounts, thermal_mesh, photosynthetic_radiance, submerged_mask, interaction_rates, photosynthetic_rates, saturation_irradiance)
    result_dimensions = zonal_boundary_speed.shape
    return (zonal_transport.reshape(result_dimensions), meridional_transport.reshape(result_dimensions), thermal_mesh.reshape(result_dimensions), brine_values.reshape(result_dimensions), tracer_amounts)
```

```python
import functools

import jax
import jax.numpy as jnp
from jax import lax
from jax.experimental import pallas as pl
from jax.experimental.pallas import tpu as pltpu
from jax.sharding import PartitionSpec as P

STEPS = 2
NG = 4
NT = 19
F32 = jnp.float32
NF = 6


def roll(x, shift, axis):
    return pltpu.roll(x, shift % x.shape[axis], axis)


def kernel(
    nx, ny,
    u_hbm, v_hbm, t_hbm, s_hbm, q_hbm, c_hbm, dep_hbm, sol_hbm, a_s, ph_s, sat_s, pig_s,
    ou, ov, ot, osl, oc,
    cin, oc_in, dep, sol, cs, hs, hn, zup_s, zdn_s, zup_r, zdn_r, xe_s, xw_s, xe_r, xw_r,
    ps, pf, fs, fr, ush, uw, vsh, vsr, dpx, ops, mix, cw, ce, cu, cd,
    loc, psend, precv, fsend, frecv, esend, erecv, nsend, nrecv, hsend, hrecv, dsend, drecv,
):
    b = lax.axis_index("grp")
    ix = lax.axis_index("gx")
    iy = lax.axis_index("gy")
    east, west = lax.rem(ix + 1, nx), lax.rem(ix + nx - 1, nx)
    north, south = lax.rem(iy + 1, ny), lax.rem(iy + ny - 1, ny)
    peers = [lax.rem(b + k, NG) for k in (2, 3, 1)]

    barrier = pltpu.get_barrier_semaphore()
    for g in range(NG):
        for dev in ({"grp": g, "gy": north}, {"grp": g, "gy": south}, {"grp": g, "gx": east}, {"grp": g, "gx": west}):
            pl.semaphore_signal(barrier, inc=1, device_id=dev)
    for g in peers:
        pl.semaphore_signal(barrier, inc=1, device_id={"grp": g})

    loads = [pltpu.make_async_copy(c_hbm, cin, loc.at[0])]
    for n, ref in enumerate((u_hbm, v_hbm, t_hbm, s_hbm, q_hbm)):
        loads.append(pltpu.make_async_copy(ref, oc_in.at[n], loc.at[1 + n]))
    loads.append(pltpu.make_async_copy(dep_hbm, dep, loc.at[6]))
    loads.append(pltpu.make_async_copy(sol_hbm, sol, loc.at[7]))
    for copy in loads:
        copy.start()

    lane8 = lax.broadcasted_iota(jnp.int32, (8, 128), 1)
    lane32 = lax.broadcasted_iota(jnp.int32, (32, 128), 1)
    row32 = lax.broadcasted_iota(jnp.int32, (32, 128), 0)
    sends = []

    def send(src, dst, ssem, rsem, dev):
        copy = pltpu.make_async_remote_copy(src, dst, ssem, rsem, device_id=dev, device_id_type=pl.DeviceIdType.MESH)
        copy.start()
        sends.append(copy)

    def arrived(dst, ssem, rsem):
        pltpu.make_async_remote_copy(dst, dst, ssem, rsem, device_id={"grp": peers[0]}, device_id_type=pl.DeviceIdType.MESH).wait_recv()

    def publish(t):
        pig = jnp.zeros((32, 128), F32)
        for i in range(NT):
            pig = pig + pig_s[i] * cs[t, i]
        for r in range(NG):
            ps[t, r] = pig[8 * r : 8 * r + 8]
        pf[t, pl.ds(pl.multiple_of(b * 8, 8), 8), :] = ps[t, b]
        if t == 0:
            pl.semaphore_wait(barrier, 4 * NG + NG - 1)
        mine = pf.at[t, pl.ds(pl.multiple_of(b * 8, 8), 8), :]
        for k, g in enumerate(peers):
            send(ps.at[t, g], mine, psend.at[t, k], precv.at[t, b], {"grp": g})
        if t == 0:
            for k, dev in enumerate(({"gx": west}, {"gx": east}, {"gy": south}, {"gy": north})):
                send(dep_hbm, dpx.at[k], dsend.at[k], drecv.at[k], dev)
        send(cs.at[t, :, pl.ds(24, 8), :], hs.at[t], hsend.at[t, 0], hrecv.at[t, 0], {"gy": north})
        send(cs.at[t, :, pl.ds(0, 8), :], hn.at[t], hsend.at[t, 1], hrecv.at[t, 1], {"gy": south})
        pe = jnp.zeros((32, 128), F32)
        pw = jnp.zeros((32, 128), F32)
        for i in range(NT):
            x = cs[t, i]
            pe = jnp.where(lane32 == i, roll(x, i + 1, 1), pe)
            pw = jnp.where(lane32 == i, roll(x, i, 1) if i else x, pw)
        xe_s[t] = pe
        xw_s[t] = pw
        send(xe_s.at[t], xw_r.at[t], hsend.at[t, 2], hrecv.at[t, 2], {"gx": east})
        send(xw_s.at[t], xe_r.at[t], hsend.at[t, 3], hrecv.at[t, 3], {"gx": west})
        for i in range(NT):
            zup_s[t, i] = cs[t, i, pl.ds(7, NG, stride=8), :]
            zdn_s[t, i] = cs[t, i, pl.ds(0, NG, stride=8), :]

        @pl.when(b < NG - 1)
        def _():
            pltpu.make_async_remote_copy(zup_s.at[t], zup_r.at[t], hsend.at[t, 4], hrecv.at[t, 4], device_id={"grp": b + 1}, device_id_type=pl.DeviceIdType.MESH).start()

        @pl.when(b > 0)
        def _():
            pltpu.make_async_remote_copy(zdn_s.at[t], zdn_r.at[t], hsend.at[t, 5], hrecv.at[t, 5], device_id={"grp": b - 1}, device_id_type=pl.DeviceIdType.MESH).start()

    def local_terms(t):
        def mixing(i, _):
            acc = a_s[i, 0] * cs[t, 0]
            for j in range(1, NT):
                acc = acc + a_s[i, j] * cs[t, j]
            mix[i] = acc
            x = cs[t, i]
            cw[i] = roll(x, 1, 1)
            ce[i] = roll(x, 127, 1)
            cu[i] = roll(x, 1, 0)
            cd[i] = roll(x, 31, 0)
            return 0

        lax.fori_loop(0, NT, mixing, 0)

    def columns(t):
        for k, g in enumerate(peers):
            dst = pf.at[t, pl.ds(pl.multiple_of(g * 8, 8), 8), :]
            arrived(dst, psend.at[t, k], precv.at[t, g])
        att = 0.01 + 0.05 * pf[t]
        cum = att
        for s in (1, 2, 4, 8, 16):
            cum = cum + jnp.where(row32 >= s, roll(cum, s, 0), 0.0)
        top = sol[pl.ds(b, 1), :] * jnp.exp(att - cum)
        heating = top * (1.0 - jnp.exp(-att))
        par = top * jnp.exp(-0.5 * att)
        wet = (row32 < dep[pl.ds(b, 1), :]).astype(F32)
        src = oc_in if t == 0 else None
        if t == 0:
            u, v, temp, sal = (oc_in[n] for n in range(4))
        else:
            u, v, temp, sal = ou[...], ov[...], ot[...], osl[...]
        quiet = oc_in[4]
        temp = temp + 5.0 * heating * wet
        rho = 0.8 * sal - 0.2 * temp
        strat = roll(rho, 31, 0) - rho
        face = (0.5 * (quiet + roll(quiet, 31, 0)) + 0.15 * jax.nn.sigmoid(-strat)) * roll(wet, 31, 0)
        face = jnp.where(row32 < 31, face, 0.0)

        def stir(x):
            flux = face * (roll(x, 31, 0) - x)
            return x + flux - roll(flux, 1, 0)

        u, v, temp, sal = stir(u), stir(v), stir(temp), stir(sal)
        above = roll(face, 1, 0)
        ou[...] = u
        ov[...] = v
        ot[...] = temp
        osl[...] = sal
        warm = jnp.exp(0.0633 * (temp - 20.0))
        for n, x in enumerate((u, v, warm, face, above, par)):
            for g in range(NG):
                fs[t, g, n] = x[8 * g : 8 * g + 8]
        fr[t, b] = fs[t, b]
        ush[t] = roll(u, 1, 1)
        vsh[t] = v
        for k, g in enumerate(peers):
            send(fs.at[t, g], fr.at[t, b], fsend.at[t, k], frecv.at[t, b], {"grp": g})

        @pl.when(b == NG - 1)
        def _():
            for g in range(NG):
                pltpu.make_async_remote_copy(vsh.at[t, pl.ds(8 * g, 8), :], vsr.at[t], nsend.at[t, g], nrecv.at[t], device_id={"grp": g, "gy": north}, device_id_type=pl.DeviceIdType.MESH).start()

        for g in range(NG):
            send(ush.at[t, pl.ds(8 * g, 8), :], uw.at[t, b], esend.at[t, g], erecv.at[t, b], {"grp": g, "gx": east})

    def openings():
        for k in range(4):
            arrived(dpx.at[k], dsend.at[k], drecv.at[k])
        level = (lax.broadcasted_iota(jnp.int32, (8, 128), 0) + 8 * b).astype(F32)

        def wet_of(rows):
            return jnp.where(level < jnp.broadcast_to(rows, (8, 128)), 1.0, 0.0)

        def row(ref, r):
            return jnp.broadcast_to(ref[r : r + 1, :].astype(F32), (8, 128))

        own = [row(dep, r) for r in range(NG)]
        wets = [wet_of(x) for x in own]
        inside_e = (ix < nx - 1).astype(F32)
        inside_w = (ix > 0).astype(F32)
        inside_n = (iy < ny - 1).astype(F32)
        inside_s = (iy > 0).astype(F32)
        wet_n = wet_of(row(dpx.at[2], 0)) * inside_n
        wet_s = wet_of(row(dpx.at[3], NG - 1)) * inside_s
        for r in range(NG):
            wet_e = jnp.where(lane8 == 127, roll(wet_of(row(dpx.at[0], r)), 127, 1) * inside_e, roll(wets[r], 127, 1))
            wet_w = jnp.where(lane8 == 0, roll(wet_of(row(dpx.at[1], r)), 1, 1) * inside_w, roll(wets[r], 1, 1))
            ops[0, r] = wets[r] * wet_e
            ops[1, r] = wets[r] * wet_w
            ops[2, r] = wets[r] * (wets[r + 1] if r < NG - 1 else wet_n)
            ops[3, r] = wets[r] * (wets[r - 1] if r > 0 else wet_s)
            ops[4, r] = 0.5 * wets[r]

    def halos(t):
        arrived(hs.at[t], hsend.at[t, 0], hrecv.at[t, 0])
        arrived(hn.at[t], hsend.at[t, 1], hrecv.at[t, 1])
        arrived(xw_r.at[t], hsend.at[t, 2], hrecv.at[t, 2])
        arrived(xe_r.at[t], hsend.at[t, 3], hrecv.at[t, 3])
        pw = xw_r[t]
        pe = xe_r[t]
        for i in range(NT):
            cw[i] = jnp.where(lane32 == 0, roll(pw, 128 - i, 1) if i else pw, cw[i])
            ce[i] = jnp.where(lane32 == 127, roll(pe, 127 - i, 1), ce[i])

        @pl.when(b > 0)
        def _():
            arrived(zup_r.at[t], hsend.at[t, 4], hrecv.at[t, 4])
            for i in range(NT):
                cu[i, pl.ds(0, NG, stride=8), :] = zup_r[t, i]

        @pl.when(b < NG - 1)
        def _():
            arrived(zdn_r.at[t], hsend.at[t, 5], hrecv.at[t, 5])
            for i in range(NT):
                cd[i, pl.ds(7, NG, stride=8), :] = zdn_r[t, i]

    def update(t):
        for k, g in enumerate(peers):
            arrived(fr.at[t, g], fsend.at[t, k], frecv.at[t, g])
        for g in range(NG):
            arrived(uw.at[t, g], esend.at[t, g], erecv.at[t, g])
        arrived(vsr.at[t], nsend.at[t, 0], nrecv.at[t])
        for r in range(NG):
            u, v, warm, d, dm, par = (fr[t, r, n] for n in range(NF))
            uwest = jnp.where(lane8 == 0, uw[t, r], roll(u, 1, 1))
            vsouth = fr[t, r - 1, 1] if r > 0 else vsr[t]
            a_e = ops[0, r] * (jnp.maximum(u, 0.0) + 0.05)
            b_e = ops[0, r] * (0.05 - jnp.minimum(u, 0.0))
            a_w = ops[1, r] * (jnp.maximum(uwest, 0.0) + 0.05)
            b_w = ops[1, r] * (0.05 - jnp.minimum(uwest, 0.0))
            a_n = ops[2, r] * (jnp.maximum(v, 0.0) + 0.05)
            b_n = ops[2, r] * (0.05 - jnp.minimum(v, 0.0))
            a_s_ = ops[3, r] * (jnp.maximum(vsouth, 0.0) + 0.05)
            b_s = ops[3, r] * (0.05 - jnp.minimum(vsouth, 0.0))
            k0 = 1.0 - a_e - b_w - a_n - b_s - d - dm
            half = ops[4, r]
            warm = half * warm
            parw = half * par
            rows = pl.ds(8 * r, 8)

            def one(i, _):
                x = cs[t, i, rows, :]
                up = cs[t, i, pl.ds(8 * r + 8, 8), :] if r < NG - 1 else hn[t, i]
                dn = cs[t, i, pl.ds(8 * r - 8, 8), :] if r > 0 else hs[t, i]
                grow = k0 + ph_s[i] * parw / (par + sat_s[i])
                new = (
                    grow * x
                    + (b_e * ce[i, rows, :] + a_w * cw[i, rows, :])
                    + (b_n * up + a_s_ * dn)
                    + (d * cd[i, rows, :] + dm * cu[i, rows, :])
                    + warm * mix[i, rows, :]
                )
                if t == STEPS - 1:
                    oc[pl.ds(i * 32 + r, 8, stride=4), :] = new
                else:
                    cs[t + 1, i, rows, :] = new
                return 0

            lax.fori_loop(0, NT, one, 0, unroll=True)

    loads[0].wait()
    for i in range(NT):
        for r in range(NG):
            cs[0, i, pl.ds(8 * r, 8), :] = cin[pl.ds(i * 32 + r, 8, stride=4), :]
    loads[6].wait()
    publish(0)
    for copy in loads[1:6] + loads[7:]:
        copy.wait()
    local_terms(0)
    openings()
    columns(0)
    halos(0)
    update(0)
    publish(1)
    local_terms(1)
    columns(1)
    halos(1)
    update(1)

    for copy in sends:
        copy.wait_send()
    for t in range(STEPS):

        @pl.when(b < NG - 1)
        def _():
            pltpu.make_async_remote_copy(zup_s.at[t], zup_r.at[t], hsend.at[t, 4], hrecv.at[t, 4], device_id={"grp": b + 1}, device_id_type=pl.DeviceIdType.MESH).wait_send()

        @pl.when(b > 0)
        def _():
            pltpu.make_async_remote_copy(zdn_s.at[t], zdn_r.at[t], hsend.at[t, 5], hrecv.at[t, 5], device_id={"grp": b - 1}, device_id_type=pl.DeviceIdType.MESH).wait_send()

        @pl.when(b == NG - 1)
        def _():
            for g in range(NG):
                pltpu.make_async_remote_copy(vsh.at[t, pl.ds(8 * g, 8), :], vsr.at[t], nsend.at[t, g], nrecv.at[t], device_id={"grp": g, "gy": north}, device_id_type=pl.DeviceIdType.MESH).wait_send()


def per_device(nx, ny, *args):
    u, v, temp, sal, quiet, c, dep, sol, rates, photo, satur, pig = args
    shape = u.shape
    fields = [x.reshape(32, 128) for x in (u, v, temp, sal, quiet)]
    hbm = pl.BlockSpec(memory_space=pl.ANY)
    smem = pl.BlockSpec(memory_space=pltpu.SMEM)
    vmem = pl.BlockSpec(memory_space=pltpu.VMEM)
    col = jax.ShapeDtypeStruct((32, 128), F32)
    V = pltpu.VMEM
    D = pltpu.SemaphoreType.DMA
    S = STEPS
    out = pl.pallas_call(
        functools.partial(kernel, nx, ny),
        out_shape=(col, col, col, col, jax.ShapeDtypeStruct((NT * 32, 128), F32)),
        in_specs=[hbm] * 8 + [smem] * 4,
        out_specs=(vmem,) * 5,
        scratch_shapes=[
            V((NT * 32, 128), F32), V((5, 32, 128), F32), V((4, 128), jnp.int32), V((4, 128), F32),
            V((S, NT, 32, 128), F32), V((S, NT, 8, 128), F32), V((S, NT, 8, 128), F32),
            V((S, NT, 4, 128), F32), V((S, NT, 4, 128), F32), V((S, NT, 4, 128), F32), V((S, NT, 4, 128), F32),
            V((S, 32, 128), F32), V((S, 32, 128), F32), V((S, 32, 128), F32), V((S, 32, 128), F32),
            V((S, NG, 8, 128), F32), V((S, 32, 128), F32),
            V((S, NG, NF, 8, 128), F32), V((S, NG, NF, 8, 128), F32),
            V((S, 32, 128), F32), V((S, NG, 8, 128), F32), V((S, 32, 128), F32), V((S, 8, 128), F32),
            V((4, 4, 128), jnp.int32), V((5, NG, 8, 128), F32),
            V((NT, 32, 128), F32), V((NT, 32, 128), F32), V((NT, 32, 128), F32), V((NT, 32, 128), F32), V((NT, 32, 128), F32),
            D((8,)), D((S, 3)), D((S, NG)), D((S, 3)), D((S, NG)), D((S, NG)), D((S, NG)), D((S, NG)), D((S,)),
            D((S, 6)), D((S, 6)), D((4,)), D((4,)),
        ],
        compiler_params=pltpu.CompilerParams(collective_id=0, has_side_effects=True),
    )(*fields, c.reshape(NT * 32, 128), dep, sol, rates, photo, satur, pig)
    return tuple(x.reshape(shape) for x in out[:4]) + (out[4].reshape(c.shape),)


def solution(mesh):
    field = P(None, "gy", "grp", "gx")
    tracer = P(None, "grp", "gy", "gx")
    flat = P("gy", "gx")
    return jax.shard_map(
        functools.partial(per_device, mesh.shape["gx"], mesh.shape["gy"]),
        mesh=mesh,
        in_specs=(field,) * 5 + (tracer, flat, flat, P(), P(), P(), P()),
        out_specs=(field,) * 4 + (tracer,),
        check_vma=False,
    )
```

```python
import functools

import jax
import jax.numpy as jnp
from jax import lax
from jax.experimental import pallas as pl
from jax.experimental.pallas import tpu as pltpu
from jax.sharding import PartitionSpec as P

STEPS = 2
NG = 4
NT = 19
F32 = jnp.float32
NF = 6


def roll(x, shift, axis):
    return pltpu.roll(x, shift % x.shape[axis], axis)


def kernel(
    nx, ny,
    u_hbm, v_hbm, t_hbm, s_hbm, q_hbm, c_hbm, dep_hbm, sol_hbm, a_s, ph_s, sat_s, pig_s,
    ou, ov, ot, osl, oc,
    cin, oc_in, dep, sol, cs, hs, hn, zup_s, zdn_s, zup_r, zdn_r, xe_s, xw_s, xe_r, xw_r,
    ps, pf, fs, fr, ush, uw, vsh, vsr, dpx, ops, mix, cw, ce, cu, cd,
    loc, psend, precv, fsend, frecv, esend, erecv, nsend, nrecv, hsend, hrecv, dsend, drecv,
):
    b = lax.axis_index("grp")
    ix = lax.axis_index("gx")
    iy = lax.axis_index("gy")
    has_e, has_w, has_n, has_s = ix < nx - 1, ix > 0, iy < ny - 1, iy > 0
    east, west, north, south = {"gx": ix + 1}, {"gx": ix - 1}, {"gy": iy + 1}, {"gy": iy - 1}
    sides = ((has_w, west), (has_e, east), (has_s, south), (has_n, north))
    peers = [lax.rem(b + k, NG) for k in (2, 3, 1)]

    barrier = pltpu.get_barrier_semaphore()
    for there, dev in sides:

        @pl.when(there)
        def _():
            for g in range(NG):
                pl.semaphore_signal(barrier, inc=1, device_id={"grp": g, **dev})

    for g in peers:
        pl.semaphore_signal(barrier, inc=1, device_id={"grp": g})

    loads = [pltpu.make_async_copy(c_hbm, cin, loc.at[0])]
    for n, ref in enumerate((u_hbm, v_hbm, t_hbm, s_hbm, q_hbm)):
        loads.append(pltpu.make_async_copy(ref, oc_in.at[n], loc.at[1 + n]))
    loads.append(pltpu.make_async_copy(dep_hbm, dep, loc.at[6]))
    loads.append(pltpu.make_async_copy(sol_hbm, sol, loc.at[7]))
    for copy in loads:
        copy.start()

    lane8 = lax.broadcasted_iota(jnp.int32, (8, 128), 1)
    lane32 = lax.broadcasted_iota(jnp.int32, (32, 128), 1)
    row32 = lax.broadcasted_iota(jnp.int32, (32, 128), 0)
    sends = []

    def send(src, dst, ssem, rsem, dev, there=None):
        copy = pltpu.make_async_remote_copy(src, dst, ssem, rsem, device_id=dev, device_id_type=pl.DeviceIdType.MESH)
        sends.append((there, copy))
        if there is None:
            copy.start()
        else:
            pl.when(there)(copy.start)

    def arrived(dst, ssem, rsem, there=None):
        copy = pltpu.make_async_remote_copy(dst, dst, ssem, rsem, device_id={"grp": peers[0]}, device_id_type=pl.DeviceIdType.MESH)
        if there is None:
            copy.wait_recv()
        else:
            pl.when(there)(copy.wait_recv)

    for there, refs in ((has_w, (uw, xw_r)), (has_e, (xe_r,)), (has_s, (vsr, hs)), (has_n, (hn,))):

        @pl.when(jnp.logical_not(there))
        def _():
            for ref in refs:
                ref[...] = jnp.zeros_like(ref)

    for k, (there, _) in enumerate(sides):

        @pl.when(jnp.logical_not(there))
        def _():
            dpx[k] = jnp.zeros((4, 128), jnp.int32)

    def publish(t):
        pig = jnp.zeros((32, 128), F32)
        for i in range(NT):
            pig = pig + pig_s[i] * cs[t, i]
        for r in range(NG):
            ps[t, r] = pig[8 * r : 8 * r + 8]
        pf[t, pl.ds(pl.multiple_of(b * 8, 8), 8), :] = ps[t, b]
        if t == 0:
            pl.semaphore_wait(barrier, NG - 1 + NG * sum(there.astype(jnp.int32) for there, _ in sides))
        mine = pf.at[t, pl.ds(pl.multiple_of(b * 8, 8), 8), :]
        for k, g in enumerate(peers):
            send(ps.at[t, g], mine, psend.at[t, k], precv.at[t, b], {"grp": g})
        if t == 0:
            for k, (there, dev) in enumerate(sides):
                send(dep_hbm, dpx.at[k ^ 1], dsend.at[k], drecv.at[k ^ 1], dev, there)
        send(cs.at[t, :, pl.ds(24, 8), :], hs.at[t], hsend.at[t, 0], hrecv.at[t, 0], north, has_n)
        send(cs.at[t, :, pl.ds(0, 8), :], hn.at[t], hsend.at[t, 1], hrecv.at[t, 1], south, has_s)
        pe = jnp.zeros((32, 128), F32)
        pw = jnp.zeros((32, 128), F32)
        for i in range(NT):
            x = cs[t, i]
            pe = jnp.where(lane32 == i, roll(x, i + 1, 1), pe)
            pw = jnp.where(lane32 == i, roll(x, i, 1) if i else x, pw)
        xe_s[t] = pe
        xw_s[t] = pw
        send(xe_s.at[t], xw_r.at[t], hsend.at[t, 2], hrecv.at[t, 2], east, has_e)
        send(xw_s.at[t], xe_r.at[t], hsend.at[t, 3], hrecv.at[t, 3], west, has_w)
        for i in range(NT):
            zup_s[t, i] = cs[t, i, pl.ds(7, NG, stride=8), :]
            zdn_s[t, i] = cs[t, i, pl.ds(0, NG, stride=8), :]

        send(zup_s.at[t], zup_r.at[t], hsend.at[t, 4], hrecv.at[t, 4], {"grp": b + 1}, b < NG - 1)
        send(zdn_s.at[t], zdn_r.at[t], hsend.at[t, 5], hrecv.at[t, 5], {"grp": b - 1}, b > 0)

    def local_terms(t):
        def mixing(i, _):
            acc = a_s[i, 0] * cs[t, 0]
            for j in range(1, NT):
                acc = acc + a_s[i, j] * cs[t, j]
            mix[i] = acc
            x = cs[t, i]
            cw[i] = roll(x, 1, 1)
            ce[i] = roll(x, 127, 1)
            cu[i] = roll(x, 1, 0)
            cd[i] = roll(x, 31, 0)
            return 0

        lax.fori_loop(0, NT, mixing, 0)

    def columns(t):
        for k, g in enumerate(peers):
            dst = pf.at[t, pl.ds(pl.multiple_of(g * 8, 8), 8), :]
            arrived(dst, psend.at[t, k], precv.at[t, g])
        att = 0.01 + 0.05 * pf[t]
        cum = att
        for s in (1, 2, 4, 8, 16):
            cum = cum + jnp.where(row32 >= s, roll(cum, s, 0), 0.0)
        top = sol[pl.ds(b, 1), :] * jnp.exp(att - cum)
        heating = top * (1.0 - jnp.exp(-att))
        par = top * jnp.exp(-0.5 * att)
        wet = (row32 < dep[pl.ds(b, 1), :]).astype(F32)
        if t == 0:
            u, v, temp, sal = (oc_in[n] for n in range(4))
        else:
            u, v, temp, sal = ou[...], ov[...], ot[...], osl[...]
        quiet = oc_in[4]
        temp = temp + 5.0 * heating * wet
        rho = 0.8 * sal - 0.2 * temp
        strat = roll(rho, 31, 0) - rho
        face = (0.5 * (quiet + roll(quiet, 31, 0)) + 0.15 * jax.nn.sigmoid(-strat)) * roll(wet, 31, 0)
        face = jnp.where(row32 < 31, face, 0.0)

        def stir(x):
            flux = face * (roll(x, 31, 0) - x)
            return x + flux - roll(flux, 1, 0)

        u, v, temp, sal = stir(u), stir(v), stir(temp), stir(sal)
        above = roll(face, 1, 0)
        ou[...] = u
        ov[...] = v
        ot[...] = temp
        osl[...] = sal
        warm = jnp.exp(0.0633 * (temp - 20.0))
        for n, x in enumerate((u, v, warm, face, above, par)):
            for g in range(NG):
                fs[t, g, n] = x[8 * g : 8 * g + 8]
        fr[t, b] = fs[t, b]
        ush[t] = roll(u, 1, 1)
        vsh[t] = v
        for k, g in enumerate(peers):
            send(fs.at[t, g], fr.at[t, b], fsend.at[t, k], frecv.at[t, b], {"grp": g})

        for g in range(NG):
            send(vsh.at[t, pl.ds(8 * g, 8), :], vsr.at[t], nsend.at[t, g], nrecv.at[t], {"grp": g, **north}, jnp.logical_and(b == NG - 1, has_n))
            send(ush.at[t, pl.ds(8 * g, 8), :], uw.at[t, b], esend.at[t, g], erecv.at[t, b], {"grp": g, **east}, has_e)

    def openings():
        for k in range(4):
            arrived(dpx.at[k], dsend.at[k], drecv.at[k], sides[k][0])
        level = (lax.broadcasted_iota(jnp.int32, (8, 128), 0) + 8 * b).astype(F32)

        def wet_of(rows):
            return jnp.where(level < jnp.broadcast_to(rows, (8, 128)), 1.0, 0.0)

        def row(ref, r):
            return jnp.broadcast_to(ref[r : r + 1, :].astype(F32), (8, 128))

        own = [row(dep, r) for r in range(NG)]
        wets = [wet_of(x) for x in own]
        wet_n = wet_of(row(dpx.at[3], 0))
        wet_s = wet_of(row(dpx.at[2], NG - 1))
        for r in range(NG):
            wet_e = jnp.where(lane8 == 127, roll(wet_of(row(dpx.at[1], r)), 127, 1), roll(wets[r], 127, 1))
            wet_w = jnp.where(lane8 == 0, roll(wet_of(row(dpx.at[0], r)), 1, 1), roll(wets[r], 1, 1))
            ops[0, r] = wets[r] * wet_e
            ops[1, r] = wets[r] * wet_w
            ops[2, r] = wets[r] * (wets[r + 1] if r < NG - 1 else wet_n)
            ops[3, r] = wets[r] * (wets[r - 1] if r > 0 else wet_s)
            ops[4, r] = 0.5 * wets[r]

    def halos(t):
        arrived(hs.at[t], hsend.at[t, 0], hrecv.at[t, 0], has_s)
        arrived(hn.at[t], hsend.at[t, 1], hrecv.at[t, 1], has_n)
        arrived(xw_r.at[t], hsend.at[t, 2], hrecv.at[t, 2], has_w)
        arrived(xe_r.at[t], hsend.at[t, 3], hrecv.at[t, 3], has_e)
        pw = xw_r[t]
        pe = xe_r[t]
        for i in range(NT):
            cw[i] = jnp.where(lane32 == 0, roll(pw, 128 - i, 1) if i else pw, cw[i])
            ce[i] = jnp.where(lane32 == 127, roll(pe, 127 - i, 1), ce[i])

        @pl.when(b > 0)
        def _():
            arrived(zup_r.at[t], hsend.at[t, 4], hrecv.at[t, 4])
            for i in range(NT):
                cu[i, pl.ds(0, NG, stride=8), :] = zup_r[t, i]

        @pl.when(b < NG - 1)
        def _():
            arrived(zdn_r.at[t], hsend.at[t, 5], hrecv.at[t, 5])
            for i in range(NT):
                cd[i, pl.ds(7, NG, stride=8), :] = zdn_r[t, i]

    def update(t):
        for k, g in enumerate(peers):
            arrived(fr.at[t, g], fsend.at[t, k], frecv.at[t, g])
        for g in range(NG):
            arrived(uw.at[t, g], esend.at[t, g], erecv.at[t, g], has_w)
        arrived(vsr.at[t], nsend.at[t, 0], nrecv.at[t], has_s)
        for r in range(NG):
            u, v, warm, d, dm, par = (fr[t, r, n] for n in range(NF))
            uwest = jnp.where(lane8 == 0, uw[t, r], roll(u, 1, 1))
            vsouth = fr[t, r - 1, 1] if r > 0 else vsr[t]
            a_e = ops[0, r] * (jnp.maximum(u, 0.0) + 0.05)
            b_e = ops[0, r] * (0.05 - jnp.minimum(u, 0.0))
            a_w = ops[1, r] * (jnp.maximum(uwest, 0.0) + 0.05)
            b_w = ops[1, r] * (0.05 - jnp.minimum(uwest, 0.0))
            a_n = ops[2, r] * (jnp.maximum(v, 0.0) + 0.05)
            b_n = ops[2, r] * (0.05 - jnp.minimum(v, 0.0))
            a_s_ = ops[3, r] * (jnp.maximum(vsouth, 0.0) + 0.05)
            b_s = ops[3, r] * (0.05 - jnp.minimum(vsouth, 0.0))
            k0 = 1.0 - a_e - b_w - a_n - b_s - d - dm
            half = ops[4, r]
            warm = half * warm
            parw = half * par
            rows = pl.ds(8 * r, 8)

            def one(i, _):
                x = cs[t, i, rows, :]
                up = cs[t, i, pl.ds(8 * r + 8, 8), :] if r < NG - 1 else hn[t, i]
                dn = cs[t, i, pl.ds(8 * r - 8, 8), :] if r > 0 else hs[t, i]
                grow = k0 + ph_s[i] * parw / (par + sat_s[i])
                new = (
                    grow * x
                    + (b_e * ce[i, rows, :] + a_w * cw[i, rows, :])
                    + (b_n * up + a_s_ * dn)
                    + (d * cd[i, rows, :] + dm * cu[i, rows, :])
                    + warm * mix[i, rows, :]
                )
                if t == STEPS - 1:
                    oc[pl.ds(i * 32 + r, 8, stride=4), :] = new
                else:
                    cs[t + 1, i, rows, :] = new
                return 0

            lax.fori_loop(0, NT, one, 0, unroll=True)

    loads[0].wait()
    for i in range(NT):
        for r in range(NG):
            cs[0, i, pl.ds(8 * r, 8), :] = cin[pl.ds(i * 32 + r, 8, stride=4), :]
    loads[6].wait()
    publish(0)
    for copy in loads[1:6] + loads[7:]:
        copy.wait()
    local_terms(0)
    openings()
    columns(0)
    halos(0)
    update(0)
    publish(1)
    local_terms(1)
    columns(1)
    halos(1)
    update(1)

    for there, copy in sends:
        if there is None:
            copy.wait_send()
        else:
            pl.when(there)(copy.wait_send)


def per_device(nx, ny, *args):
    u, v, temp, sal, quiet, c, dep, sol, rates, photo, satur, pig = args
    shape = u.shape
    fields = [x.reshape(32, 128) for x in (u, v, temp, sal, quiet)]
    hbm = pl.BlockSpec(memory_space=pl.ANY)
    smem = pl.BlockSpec(memory_space=pltpu.SMEM)
    vmem = pl.BlockSpec(memory_space=pltpu.VMEM)
    col = jax.ShapeDtypeStruct((32, 128), F32)
    V = pltpu.VMEM
    D = pltpu.SemaphoreType.DMA
    S = STEPS
    out = pl.pallas_call(
        functools.partial(kernel, nx, ny),
        out_shape=(col, col, col, col, jax.ShapeDtypeStruct((NT * 32, 128), F32)),
        in_specs=[hbm] * 8 + [smem] * 4,
        out_specs=(vmem,) * 5,
        scratch_shapes=[
            V((NT * 32, 128), F32), V((5, 32, 128), F32), V((4, 128), jnp.int32), V((4, 128), F32),
            V((S, NT, 32, 128), F32), V((S, NT, 8, 128), F32), V((S, NT, 8, 128), F32),
            V((S, NT, 4, 128), F32), V((S, NT, 4, 128), F32), V((S, NT, 4, 128), F32), V((S, NT, 4, 128), F32),
            V((S, 32, 128), F32), V((S, 32, 128), F32), V((S, 32, 128), F32), V((S, 32, 128), F32),
            V((S, NG, 8, 128), F32), V((S, 32, 128), F32),
            V((S, NG, NF, 8, 128), F32), V((S, NG, NF, 8, 128), F32),
            V((S, 32, 128), F32), V((S, NG, 8, 128), F32), V((S, 32, 128), F32), V((S, 8, 128), F32),
            V((4, 4, 128), jnp.int32), V((5, NG, 8, 128), F32),
            V((NT, 32, 128), F32), V((NT, 32, 128), F32), V((NT, 32, 128), F32), V((NT, 32, 128), F32), V((NT, 32, 128), F32),
            D((8,)), D((S, 3)), D((S, NG)), D((S, 3)), D((S, NG)), D((S, NG)), D((S, NG)), D((S, NG)), D((S,)),
            D((S, 6)), D((S, 6)), D((4,)), D((4,)),
        ],
        compiler_params=pltpu.CompilerParams(collective_id=0, has_side_effects=True),
    )(*fields, c.reshape(NT * 32, 128), dep, sol, rates, photo, satur, pig)
    return tuple(x.reshape(shape) for x in out[:4]) + (out[4].reshape(c.shape),)


def solution(mesh):
    field = P(None, "gy", "grp", "gx")
    tracer = P(None, "grp", "gy", "gx")
    flat = P("gy", "gx")
    return jax.shard_map(
        functools.partial(per_device, mesh.shape["gx"], mesh.shape["gy"]),
        mesh=mesh,
        in_specs=(field,) * 5 + (tracer, flat, flat, P(), P(), P(), P()),
        out_specs=(field,) * 4 + (tracer,),
        check_vma=False,
    )
```

```python
import functools

import jax
import jax.numpy as jnp
from jax import lax
from jax.experimental import pallas as pl
from jax.experimental.pallas import tpu as pltpu
from jax.sharding import PartitionSpec as P

STEPS = 2
NG = 4
NT = 19
F32 = jnp.float32
NF = 6


def roll(x, shift, axis):
    return pltpu.roll(x, shift % x.shape[axis], axis)


def kernel(
    nx, ny,
    u_hbm, v_hbm, t_hbm, s_hbm, q_hbm, c_hbm, dep_hbm, sol_hbm, a_hbm, ph_hbm, sat_hbm, pig_hbm,
    ou, ov, ot, osl, oc,
    a_s, ph_s, sat_s, pig_s, cin, oc_in, dep, sol, cs, hs, hn, zup_s, zdn_s, zup_r, zdn_r, xe_s, xw_s, xe_r, xw_r,
    ps, pf, fs, fr, ush, uw, vsh, vsr, dpx, ops, mix, cw, ce, cu, cd,
    loc, psend, precv, fsend, frecv, esend, erecv, nsend, nrecv, hsend, hrecv, dsend, drecv,
):
    b = lax.axis_index("grp")
    ix = lax.axis_index("gx")
    iy = lax.axis_index("gy")
    has_e, has_w, has_n, has_s = ix < nx - 1, ix > 0, iy < ny - 1, iy > 0
    east, west, north, south = {"gx": ix + 1}, {"gx": ix - 1}, {"gy": iy + 1}, {"gy": iy - 1}
    sides = ((has_w, west), (has_e, east), (has_s, south), (has_n, north))
    peers = [lax.rem(b + k, NG) for k in (2, 3, 1)]

    barrier = pltpu.get_barrier_semaphore()
    for there, dev in sides:

        @pl.when(there)
        def _():
            for g in range(NG):
                pl.semaphore_signal(barrier, inc=1, device_id={"grp": g, **dev})

    for g in peers:
        pl.semaphore_signal(barrier, inc=1, device_id={"grp": g})

    loads = [pltpu.make_async_copy(c_hbm, cin, loc.at[0])]
    for n, ref in enumerate((u_hbm, v_hbm, t_hbm, s_hbm, q_hbm)):
        loads.append(pltpu.make_async_copy(ref, oc_in.at[n], loc.at[1 + n]))
    loads.append(pltpu.make_async_copy(dep_hbm, dep, loc.at[6]))
    loads.append(pltpu.make_async_copy(sol_hbm, sol, loc.at[7]))
    for n, (ref, dst) in enumerate(((pig_hbm, pig_s), (a_hbm, a_s), (ph_hbm, ph_s), (sat_hbm, sat_s))):
        loads.append(pltpu.make_async_copy(ref, dst, loc.at[8 + n]))
    for copy in loads:
        copy.start()

    lane8 = lax.broadcasted_iota(jnp.int32, (8, 128), 1)
    lane32 = lax.broadcasted_iota(jnp.int32, (32, 128), 1)
    row32 = lax.broadcasted_iota(jnp.int32, (32, 128), 0)
    sends = []

    def send(src, dst, ssem, rsem, dev, there=None):
        copy = pltpu.make_async_remote_copy(src, dst, ssem, rsem, device_id=dev, device_id_type=pl.DeviceIdType.MESH)
        sends.append((there, copy))
        if there is None:
            copy.start()
        else:
            pl.when(there)(copy.start)

    def arrived(dst, ssem, rsem, there=None):
        copy = pltpu.make_async_remote_copy(dst, dst, ssem, rsem, device_id={"grp": peers[0]}, device_id_type=pl.DeviceIdType.MESH)
        if there is None:
            copy.wait_recv()
        else:
            pl.when(there)(copy.wait_recv)

    for there, refs in ((has_w, (uw, xw_r)), (has_e, (xe_r,)), (has_s, (vsr, hs)), (has_n, (hn,))):

        @pl.when(jnp.logical_not(there))
        def _():
            for ref in refs:
                ref[...] = jnp.zeros_like(ref)

    for k, (there, _) in enumerate(sides):

        @pl.when(jnp.logical_not(there))
        def _():
            dpx[k] = jnp.zeros((4, 128), jnp.int32)

    def publish(t):
        pig = jnp.zeros((32, 128), F32)
        for i in range(NT):
            pig = pig + pig_s[i] * cs[t, i]
        for r in range(NG):
            ps[t, r] = pig[8 * r : 8 * r + 8]
        pf[t, pl.ds(pl.multiple_of(b * 8, 8), 8), :] = ps[t, b]
        if t == 0:
            pl.semaphore_wait(barrier, NG - 1 + NG * sum(there.astype(jnp.int32) for there, _ in sides))
        mine = pf.at[t, pl.ds(pl.multiple_of(b * 8, 8), 8), :]
        for k, g in enumerate(peers):
            send(ps.at[t, g], mine, psend.at[t, k], precv.at[t, b], {"grp": g})
        if t == 0:
            for k, (there, dev) in enumerate(sides):
                send(dep_hbm, dpx.at[k ^ 1], dsend.at[k], drecv.at[k ^ 1], dev, there)
        send(cs.at[t, :, pl.ds(24, 8), :], hs.at[t], hsend.at[t, 0], hrecv.at[t, 0], north, has_n)
        send(cs.at[t, :, pl.ds(0, 8), :], hn.at[t], hsend.at[t, 1], hrecv.at[t, 1], south, has_s)
        pe = jnp.zeros((32, 128), F32)
        pw = jnp.zeros((32, 128), F32)
        for i in range(NT):
            x = cs[t, i]
            pe = jnp.where(lane32 == i, roll(x, i + 1, 1), pe)
            pw = jnp.where(lane32 == i, roll(x, i, 1) if i else x, pw)
        xe_s[t] = pe
        xw_s[t] = pw
        send(xe_s.at[t], xw_r.at[t], hsend.at[t, 2], hrecv.at[t, 2], east, has_e)
        send(xw_s.at[t], xe_r.at[t], hsend.at[t, 3], hrecv.at[t, 3], west, has_w)
        for i in range(NT):
            zup_s[t, i] = cs[t, i, pl.ds(7, NG, stride=8), :]
            zdn_s[t, i] = cs[t, i, pl.ds(0, NG, stride=8), :]

        send(zup_s.at[t], zup_r.at[t], hsend.at[t, 4], hrecv.at[t, 4], {"grp": b + 1}, b < NG - 1)
        send(zdn_s.at[t], zdn_r.at[t], hsend.at[t, 5], hrecv.at[t, 5], {"grp": b - 1}, b > 0)

    def local_terms(t):
        def mixing(i, _):
            acc = a_s[i, 0] * cs[t, 0]
            for j in range(1, NT):
                acc = acc + a_s[i, j] * cs[t, j]
            mix[i] = acc
            x = cs[t, i]
            cw[i] = roll(x, 1, 1)
            ce[i] = roll(x, 127, 1)
            cu[i] = roll(x, 1, 0)
            cd[i] = roll(x, 31, 0)
            return 0

        lax.fori_loop(0, NT, mixing, 0)

    def columns(t):
        for k, g in enumerate(peers):
            dst = pf.at[t, pl.ds(pl.multiple_of(g * 8, 8), 8), :]
            arrived(dst, psend.at[t, k], precv.at[t, g])
        att = 0.01 + 0.05 * pf[t]
        cum = att
        for s in (1, 2, 4, 8, 16):
            cum = cum + jnp.where(row32 >= s, roll(cum, s, 0), 0.0)
        top = sol[pl.ds(b, 1), :] * jnp.exp(att - cum)
        heating = top * (1.0 - jnp.exp(-att))
        par = top * jnp.exp(-0.5 * att)
        wet = (row32 < dep[pl.ds(b, 1), :]).astype(F32)
        if t == 0:
            u, v, temp, sal = (oc_in[n] for n in range(4))
        else:
            u, v, temp, sal = ou[...], ov[...], ot[...], osl[...]
        quiet = oc_in[4]
        temp = temp + 5.0 * heating * wet
        rho = 0.8 * sal - 0.2 * temp
        strat = roll(rho, 31, 0) - rho
        face = (0.5 * (quiet + roll(quiet, 31, 0)) + 0.15 * jax.nn.sigmoid(-strat)) * roll(wet, 31, 0)
        face = jnp.where(row32 < 31, face, 0.0)

        def stir(x):
            flux = face * (roll(x, 31, 0) - x)
            return x + flux - roll(flux, 1, 0)

        u, v, temp, sal = stir(u), stir(v), stir(temp), stir(sal)
        above = roll(face, 1, 0)
        ou[...] = u
        ov[...] = v
        ot[...] = temp
        osl[...] = sal
        warm = jnp.exp(0.0633 * (temp - 20.0))
        for n, x in enumerate((u, v, warm, face, above, par)):
            for g in range(NG):
                fs[t, g, n] = x[8 * g : 8 * g + 8]
        fr[t, b] = fs[t, b]
        ush[t] = roll(u, 1, 1)
        vsh[t] = v
        for k, g in enumerate(peers):
            send(fs.at[t, g], fr.at[t, b], fsend.at[t, k], frecv.at[t, b], {"grp": g})

        for g in range(NG):
            send(vsh.at[t, pl.ds(8 * g, 8), :], vsr.at[t], nsend.at[t, g], nrecv.at[t], {"grp": g, **north}, jnp.logical_and(b == NG - 1, has_n))
            send(ush.at[t, pl.ds(8 * g, 8), :], uw.at[t, b], esend.at[t, g], erecv.at[t, b], {"grp": g, **east}, has_e)

    def openings():
        for k in range(4):
            arrived(dpx.at[k], dsend.at[k], drecv.at[k], sides[k][0])
        level = (lax.broadcasted_iota(jnp.int32, (8, 128), 0) + 8 * b).astype(F32)

        def wet_of(rows):
            return jnp.where(level < jnp.broadcast_to(rows, (8, 128)), 1.0, 0.0)

        def row(ref, r):
            return jnp.broadcast_to(ref[r : r + 1, :].astype(F32), (8, 128))

        own = [row(dep, r) for r in range(NG)]
        wets = [wet_of(x) for x in own]
        wet_n = wet_of(row(dpx.at[3], 0))
        wet_s = wet_of(row(dpx.at[2], NG - 1))
        for r in range(NG):
            wet_e = jnp.where(lane8 == 127, roll(wet_of(row(dpx.at[1], r)), 127, 1), roll(wets[r], 127, 1))
            wet_w = jnp.where(lane8 == 0, roll(wet_of(row(dpx.at[0], r)), 1, 1), roll(wets[r], 1, 1))
            ops[0, r] = wets[r] * wet_e
            ops[1, r] = wets[r] * wet_w
            ops[2, r] = wets[r] * (wets[r + 1] if r < NG - 1 else wet_n)
            ops[3, r] = wets[r] * (wets[r - 1] if r > 0 else wet_s)
            ops[4, r] = 0.5 * wets[r]

    def halos(t):
        arrived(hs.at[t], hsend.at[t, 0], hrecv.at[t, 0], has_s)
        arrived(hn.at[t], hsend.at[t, 1], hrecv.at[t, 1], has_n)
        arrived(xw_r.at[t], hsend.at[t, 2], hrecv.at[t, 2], has_w)
        arrived(xe_r.at[t], hsend.at[t, 3], hrecv.at[t, 3], has_e)
        pw = xw_r[t]
        pe = xe_r[t]
        for i in range(NT):
            cw[i] = jnp.where(lane32 == 0, roll(pw, 128 - i, 1) if i else pw, cw[i])
            ce[i] = jnp.where(lane32 == 127, roll(pe, 127 - i, 1), ce[i])

        @pl.when(b > 0)
        def _():
            arrived(zup_r.at[t], hsend.at[t, 4], hrecv.at[t, 4])
            for i in range(NT):
                cu[i, pl.ds(0, NG, stride=8), :] = zup_r[t, i]

        @pl.when(b < NG - 1)
        def _():
            arrived(zdn_r.at[t], hsend.at[t, 5], hrecv.at[t, 5])
            for i in range(NT):
                cd[i, pl.ds(7, NG, stride=8), :] = zdn_r[t, i]

    def update(t):
        for k, g in enumerate(peers):
            arrived(fr.at[t, g], fsend.at[t, k], frecv.at[t, g])
        for g in range(NG):
            arrived(uw.at[t, g], esend.at[t, g], erecv.at[t, g], has_w)
        arrived(vsr.at[t], nsend.at[t, 0], nrecv.at[t], has_s)
        for r in range(NG):
            u, v, warm, d, dm, par = (fr[t, r, n] for n in range(NF))
            uwest = jnp.where(lane8 == 0, uw[t, r], roll(u, 1, 1))
            vsouth = fr[t, r - 1, 1] if r > 0 else vsr[t]
            a_e = ops[0, r] * (jnp.maximum(u, 0.0) + 0.05)
            b_e = ops[0, r] * (0.05 - jnp.minimum(u, 0.0))
            a_w = ops[1, r] * (jnp.maximum(uwest, 0.0) + 0.05)
            b_w = ops[1, r] * (0.05 - jnp.minimum(uwest, 0.0))
            a_n = ops[2, r] * (jnp.maximum(v, 0.0) + 0.05)
            b_n = ops[2, r] * (0.05 - jnp.minimum(v, 0.0))
            a_s_ = ops[3, r] * (jnp.maximum(vsouth, 0.0) + 0.05)
            b_s = ops[3, r] * (0.05 - jnp.minimum(vsouth, 0.0))
            k0 = 1.0 - a_e - b_w - a_n - b_s - d - dm
            half = ops[4, r]
            warm = half * warm
            parw = half * par
            rows = pl.ds(8 * r, 8)

            def one(i, _):
                x = cs[t, i, rows, :]
                up = cs[t, i, pl.ds(8 * r + 8, 8), :] if r < NG - 1 else hn[t, i]
                dn = cs[t, i, pl.ds(8 * r - 8, 8), :] if r > 0 else hs[t, i]
                grow = k0 + ph_s[i] * parw / (par + sat_s[i])
                new = (
                    grow * x
                    + (b_e * ce[i, rows, :] + a_w * cw[i, rows, :])
                    + (b_n * up + a_s_ * dn)
                    + (d * cd[i, rows, :] + dm * cu[i, rows, :])
                    + warm * mix[i, rows, :]
                )
                if t == STEPS - 1:
                    oc[pl.ds(i * 32 + r, 8, stride=4), :] = new
                else:
                    cs[t + 1, i, rows, :] = new
                return 0

            lax.fori_loop(0, NT, one, 0, unroll=True)

    loads[0].wait()
    for i in range(NT):
        for r in range(NG):
            cs[0, i, pl.ds(8 * r, 8), :] = cin[pl.ds(i * 32 + r, 8, stride=4), :]
    loads[8].wait()
    publish(0)
    for copy in loads[1:8] + loads[9:]:
        copy.wait()
    local_terms(0)
    openings()
    columns(0)
    halos(0)
    update(0)
    publish(1)
    local_terms(1)
    columns(1)
    halos(1)
    update(1)

    for there, copy in sends:
        if there is None:
            copy.wait_send()
        else:
            pl.when(there)(copy.wait_send)


def write_out(*refs):
    n = (len(refs) - 1) // 2
    copies = [pltpu.make_async_copy(refs[k], refs[n + k], refs[-1].at[k]) for k in range(n)]
    for copy in copies:
        copy.start()
    for copy in copies:
        copy.wait()


def per_device(nx, ny, *args):
    u, v, temp, sal, quiet, c, dep, sol, rates, photo, satur, pig = args
    shape = u.shape
    fields = [x.reshape(32, 128) for x in (u, v, temp, sal, quiet)]
    hbm = pl.BlockSpec(memory_space=pltpu.HBM)
    vmem = pl.BlockSpec(memory_space=pltpu.VMEM)
    col = jax.ShapeDtypeStruct((32, 128), F32)
    V = pltpu.VMEM
    D = pltpu.SemaphoreType.DMA
    S = STEPS
    out = pl.pallas_call(
        functools.partial(kernel, nx, ny),
        out_shape=(col, col, col, col, jax.ShapeDtypeStruct((NT * 32, 128), F32)),
        in_specs=[hbm] * 12,
        out_specs=(vmem,) * 5,
        scratch_shapes=[
            pltpu.SMEM((NT, NT), F32), pltpu.SMEM((NT,), F32), pltpu.SMEM((NT,), F32), pltpu.SMEM((NT,), F32),
            V((NT * 32, 128), F32), V((5, 32, 128), F32), V((4, 128), jnp.int32), V((4, 128), F32),
            V((S, NT, 32, 128), F32), V((S, NT, 8, 128), F32), V((S, NT, 8, 128), F32),
            V((S, NT, 4, 128), F32), V((S, NT, 4, 128), F32), V((S, NT, 4, 128), F32), V((S, NT, 4, 128), F32),
            V((S, 32, 128), F32), V((S, 32, 128), F32), V((S, 32, 128), F32), V((S, 32, 128), F32),
            V((S, NG, 8, 128), F32), V((S, 32, 128), F32),
            V((S, NG, NF, 8, 128), F32), V((S, NG, NF, 8, 128), F32),
            V((S, 32, 128), F32), V((S, NG, 8, 128), F32), V((S, 32, 128), F32), V((S, 8, 128), F32),
            V((4, 4, 128), jnp.int32), V((5, NG, 8, 128), F32),
            V((NT, 32, 128), F32), V((NT, 32, 128), F32), V((NT, 32, 128), F32), V((NT, 32, 128), F32), V((NT, 32, 128), F32),
            D((12,)), D((S, 3)), D((S, NG)), D((S, 3)), D((S, NG)), D((S, NG)), D((S, NG)), D((S, NG)), D((S,)),
            D((S, 6)), D((S, 6)), D((4,)), D((4,)),
        ],
        compiler_params=pltpu.CompilerParams(collective_id=0, has_side_effects=True, vmem_limit_bytes=16 << 20),
    )(*[pltpu.with_memory_space_constraint(x, pltpu.HBM) for x in (*fields, c.reshape(NT * 32, 128), dep, sol, rates, photo, satur, pig)])
    out = pl.pallas_call(
        write_out,
        out_shape=(col, col, col, col, jax.ShapeDtypeStruct((NT * 32, 128), F32)),
        in_specs=[vmem] * 5,
        out_specs=(hbm,) * 5,
        scratch_shapes=[D((5,))],
        compiler_params=pltpu.CompilerParams(vmem_limit_bytes=4 << 20),
    )(*out)
    return tuple(x.reshape(shape) for x in out[:4]) + (out[4].reshape(c.shape),)


def solution(mesh):
    field = P(None, "gy", "grp", "gx")
    tracer = P(None, "grp", "gy", "gx")
    flat = P("gy", "gx")
    return jax.shard_map(
        functools.partial(per_device, mesh.shape["gx"], mesh.shape["gy"]),
        mesh=mesh,
        in_specs=(field,) * 5 + (tracer, flat, flat, P(), P(), P(), P()),
        out_specs=(field,) * 4 + (tracer,),
        check_vma=False,
    )
```

```python
import functools

import jax
import jax.numpy as jnp
from jax import lax
from jax.experimental import pallas as pl
from jax.experimental.pallas import tpu as pltpu
from jax.sharding import PartitionSpec as P

STEPS = 2
NG = 4
NT = 19
F32 = jnp.float32
NF = 6


def roll(x, shift, axis):
    return pltpu.roll(x, shift % x.shape[axis], axis)


def kernel(
    nx, ny,
    u_hbm, v_hbm, t_hbm, s_hbm, q_hbm, c_hbm, dep_hbm, sol_hbm, a_hbm, ph_hbm, sat_hbm, pig_hbm,
    ou, ov, ot, osl, oc,
    a_s, ph_s, sat_s, pig_s, cin, oc_in, dep, sol, cs, hs, hn, zup_s, zdn_s, zup_r, zdn_r, xe_s, xw_s, xe_r, xw_r,
    ps, pf, fs, fr, vsh, vsr, dpx, ops, mix, cw, ce, cu, cd,
    pall, pws, pwr, psr, fs2, fr2, fqs, fqr, ep, ews, ewr, n2s, n2r, solx, wst,
    loc, psend, precv, fsend, frecv, esend, erecv, nsend, nrecv, hsend, hrecv, dsend, drecv, xsend, xrecv,
):
    b = lax.axis_index("grp")
    ix = lax.axis_index("gx")
    iy = lax.axis_index("gy")
    has_e, has_w, has_n, has_s = ix < nx - 1, ix > 0, iy < ny - 1, iy > 0
    east, west, north, south = {"gx": ix + 1}, {"gx": ix - 1}, {"gy": iy + 1}, {"gy": iy - 1}
    sides = ((has_w, west), (has_e, east), (has_s, south), (has_n, north))
    peers = [lax.rem(b + k, NG) for k in (2, 3, 1)]

    barrier = pltpu.get_barrier_semaphore()
    for there, dev in sides:

        @pl.when(there)
        def _():
            for g in range(NG):
                pl.semaphore_signal(barrier, inc=1, device_id={"grp": g, **dev})

    for g in peers:
        pl.semaphore_signal(barrier, inc=1, device_id={"grp": g})

    loads = [pltpu.make_async_copy(c_hbm, cin, loc.at[0])]
    for n, ref in enumerate((u_hbm, v_hbm, t_hbm, s_hbm, q_hbm)):
        loads.append(pltpu.make_async_copy(ref, oc_in.at[n], loc.at[1 + n]))
    loads.append(pltpu.make_async_copy(dep_hbm, dep, loc.at[6]))
    loads.append(pltpu.make_async_copy(sol_hbm, sol, loc.at[7]))
    for n, (ref, dst) in enumerate(((pig_hbm, pig_s), (a_hbm, a_s), (ph_hbm, ph_s), (sat_hbm, sat_s))):
        loads.append(pltpu.make_async_copy(ref, dst, loc.at[8 + n]))
    for copy in loads:
        copy.start()

    lane8 = lax.broadcasted_iota(jnp.int32, (8, 128), 1)
    lane32 = lax.broadcasted_iota(jnp.int32, (32, 128), 1)
    row8 = lax.broadcasted_iota(jnp.int32, (8, 128), 0)
    row16 = lax.broadcasted_iota(jnp.int32, (16, 128), 0)
    lane16 = lax.broadcasted_iota(jnp.int32, (16, 128), 1)
    row32 = lax.broadcasted_iota(jnp.int32, (32, 128), 0)
    sends = []

    def send(src, dst, ssem, rsem, dev, there=None):
        copy = pltpu.make_async_remote_copy(src, dst, ssem, rsem, device_id=dev, device_id_type=pl.DeviceIdType.MESH)
        sends.append((there, copy))
        if there is None:
            copy.start()
        else:
            pl.when(there)(copy.start)

    def arrived(dst, ssem, rsem, there=None):
        copy = pltpu.make_async_remote_copy(dst, dst, ssem, rsem, device_id={"grp": peers[0]}, device_id_type=pl.DeviceIdType.MESH)
        if there is None:
            copy.wait_recv()
        else:
            pl.when(there)(copy.wait_recv)

    for there, refs in ((has_w, (ewr, xw_r, pwr, solx.at[0])), (has_e, (xe_r,)), (has_s, (vsr, hs, n2r, psr, solx.at[1])), (has_n, (hn,))):

        @pl.when(jnp.logical_not(there))
        def _():
            for ref in refs:
                ref[...] = jnp.zeros_like(ref)

    for k, (there, _) in enumerate(sides):

        @pl.when(jnp.logical_not(there))
        def _():
            dpx[k] = jnp.zeros((4, 128), jnp.int32)

    def publish(t):
        pig = jnp.zeros((32, 128), F32)
        for i in range(NT):
            pig = pig + pig_s[i] * cs[t, i]
        for r in range(NG):
            ps[t, r] = pig[8 * r : 8 * r + 8]
        if t == 0:
            pf[pl.ds(pl.multiple_of(b * 8, 8), 8), :] = ps[t, b]
            pl.semaphore_wait(barrier, NG - 1 + NG * sum(there.astype(jnp.int32) for there, _ in sides))
            for k, g in enumerate(peers):
                send(ps.at[t, g], pf.at[pl.ds(pl.multiple_of(b * 8, 8), 8), :], psend.at[t, k], precv.at[t, b], {"grp": g})
        else:
            for k, g in enumerate(peers):
                send(ps.at[t], pall.at[b], psend.at[t, k], precv.at[t, b], {"grp": g})
            for g in range(NG):
                send(ps.at[t, NG - 1], psr.at[b], xsend.at[0, g], xrecv.at[0, b], {"grp": g, **north}, has_n)
            pack = jnp.zeros((8, 128), F32)
            for r in range(NG):
                pack = jnp.where(lane8 == r, roll(ps[t, r], r + 1, 1), pack)
            pws[...] = pack
            for g in range(NG):
                send(pws, pwr.at[b], xsend.at[1, g], xrecv.at[1, b], {"grp": g, **east}, has_e)
            pall[b] = ps[t]
        if t == 0:
            for k, (there, dev) in enumerate(sides):
                send(dep_hbm, dpx.at[k ^ 1], dsend.at[k], drecv.at[k ^ 1], dev, there)
            send(sol_hbm, solx.at[0], dsend.at[4], drecv.at[4], east, has_e)
            send(sol_hbm, solx.at[1], dsend.at[5], drecv.at[5], north, has_n)
        send(cs.at[t, :, pl.ds(24, 8), :], hs.at[t], hsend.at[t, 0], hrecv.at[t, 0], north, has_n)
        send(cs.at[t, :, pl.ds(0, 8), :], hn.at[t], hsend.at[t, 1], hrecv.at[t, 1], south, has_s)
        pe = jnp.zeros((32, 128), F32)
        pw = jnp.zeros((32, 128), F32)
        for i in range(NT):
            x = cs[t, i]
            pe = jnp.where(lane32 == i, roll(x, i + 1, 1), pe)
            pw = jnp.where(lane32 == i, roll(x, i, 1) if i else x, pw)
        xe_s[t] = pe
        xw_s[t] = pw
        send(xe_s.at[t], xw_r.at[t], hsend.at[t, 2], hrecv.at[t, 2], east, has_e)
        send(xw_s.at[t], xe_r.at[t], hsend.at[t, 3], hrecv.at[t, 3], west, has_w)
        for i in range(NT):
            zup_s[t, i] = cs[t, i, pl.ds(7, NG, stride=8), :]
            zdn_s[t, i] = cs[t, i, pl.ds(0, NG, stride=8), :]

        send(zup_s.at[t], zup_r.at[t], hsend.at[t, 4], hrecv.at[t, 4], {"grp": b + 1}, b < NG - 1)
        send(zdn_s.at[t], zdn_r.at[t], hsend.at[t, 5], hrecv.at[t, 5], {"grp": b - 1}, b > 0)

    def local_terms(t):
        def mixing(i, _):
            acc = a_s[i, 0] * cs[t, 0]
            for j in range(1, NT):
                acc = acc + a_s[i, j] * cs[t, j]
            mix[i] = acc
            x = cs[t, i]
            cw[i] = roll(x, 1, 1)
            ce[i] = roll(x, 127, 1)
            cu[i] = roll(x, 1, 0)
            cd[i] = roll(x, 31, 0)
            return 0

        lax.fori_loop(0, NT, mixing, 0)

    def bound(x):
        return min(max(x, 0), 31)

    def edges(hi, lo):
        return jnp.where(row8 == 0, jnp.broadcast_to(hi, (8, 128)), jnp.broadcast_to(lo, (8, 128)))

    def share_mixing():
        for g in range(NG):
            fqs[g, 0:8] = oc_in[4, 8 * g : 8 * g + 8]
            fqs[g, 8:16] = edges(oc_in[4, bound(8 * g + 8) : bound(8 * g + 8) + 1], oc_in[4, bound(8 * g - 1) : bound(8 * g - 1) + 1])
        for k, g in enumerate(peers):
            send(fqs.at[g], fqr.at[b], xsend.at[2, k], xrecv.at[2, b], {"grp": g})
        fqr[b] = fqs[b]

    def columns(t):
        if t == 0:
            for k, g in enumerate(peers):
                arrived(pf.at[pl.ds(pl.multiple_of(g * 8, 8), 8), :], psend.at[t, k], precv.at[t, g])
            pig = pf[...]
            u, v, temp, sal = (oc_in[n] for n in range(4))
        else:
            pig = jnp.concatenate([pall[g, b] for g in range(NG)], axis=0)
            u, v, temp, sal = ou[...], ov[...], ot[...], osl[...]
        att = 0.01 + 0.05 * pig
        cum = att
        for s in (1, 2, 4, 8, 16):
            cum = cum + jnp.where(row32 >= s, roll(cum, s, 0), 0.0)
        top = sol[pl.ds(b, 1), :] * jnp.exp(att - cum)
        heating = top * (1.0 - jnp.exp(-att))
        wet = (row32 < dep[pl.ds(b, 1), :]).astype(F32)
        quiet = oc_in[4]
        temp = temp + 5.0 * heating * wet
        rho = 0.8 * sal - 0.2 * temp
        strat = roll(rho, 31, 0) - rho
        face = (0.5 * (quiet + roll(quiet, 31, 0)) + 0.15 * jax.nn.sigmoid(-strat)) * roll(wet, 31, 0)
        face = jnp.where(row32 < 31, face, 0.0)

        def stir(x):
            flux = face * (roll(x, 31, 0) - x)
            return x + flux - roll(flux, 1, 0)

        u, v, temp, sal = stir(u), stir(v), stir(temp), stir(sal)
        if t == 0:
            par = top * jnp.exp(-0.5 * att)
            for n, x in enumerate((u, v, temp, face, roll(face, 1, 0), par)):
                for g in range(NG):
                    fs[g, n] = x[8 * g : 8 * g + 8]
            for k, g in enumerate(peers):
                send(fs.at[g], fr.at[b], fsend.at[0, k], frecv.at[0, b], {"grp": g})
            vsh[...] = v
            for g in range(NG):
                send(vsh.at[pl.ds(8 * g, 8), :], vsr, nsend.at[0, g], nrecv.at[0], {"grp": g, **north}, jnp.logical_and(b == NG - 1, has_n))
            pack = jnp.zeros((32, 128), F32)
            for n, x in enumerate((u, temp, sal, quiet)):
                pack = jnp.where(lane32 == n, roll(x, n + 1, 1), pack)
            ep[...] = pack
            for g in range(NG):
                hi, lo = bound(8 * g + 8), bound(8 * g - 1)
                ews[g, 0:8] = ep[8 * g : 8 * g + 8]
                ews[g, 8:16] = edges(ep[hi : hi + 1], ep[lo : lo + 1])
                send(ews.at[g], ewr.at[b], esend.at[g], erecv.at[b], {"grp": g, **east}, has_e)
            fr[b] = fs[b]
        ou[...] = u
        ov[...] = v
        ot[...] = temp
        osl[...] = sal

    def share_state():
        for g in range(NG):
            hi, lo = bound(8 * g + 8), bound(8 * g - 1)
            fs2[g, 0] = osl[8 * g : 8 * g + 8]
            for n, x in enumerate((ou, ov, ot, osl)):
                fs2[g, 1, 2 * n : 2 * n + 1] = x[hi : hi + 1]
                fs2[g, 1, 2 * n + 1 : 2 * n + 2] = x[lo : lo + 1]
        for k, g in enumerate(peers):
            send(fs2.at[g], fr2.at[b], fsend.at[1, k], frecv.at[1, b], {"grp": g})
        fr2[b] = fs2[b]
        quiet = oc_in.at[4]
        for g in range(NG):
            hi, lo = bound(8 * g + 8), bound(8 * g - 1)
            for n, x in enumerate((ot, osl, quiet)):
                n2s[g, n] = x[8 * g : 8 * g + 8]
            for n, x in enumerate((ov, ot, osl, quiet)):
                n2s[g, 3, 2 * n : 2 * n + 1] = x[hi : hi + 1]
                n2s[g, 3, 2 * n + 1 : 2 * n + 2] = x[lo : lo + 1]
            send(n2s.at[g], n2r, nsend.at[1, g], nrecv.at[1], {"grp": g, **north}, jnp.logical_and(b == NG - 1, has_n))

    def await_state():
        for k, g in enumerate(peers):
            arrived(fr2.at[g], fsend.at[1, k], frecv.at[1, g])
            arrived(fqr.at[g], xsend.at[2, k], xrecv.at[2, g])
        arrived(n2r, nsend.at[1, 0], nrecv.at[1], has_s)
        arrived(solx.at[0], dsend.at[4], drecv.at[4], has_w)
        arrived(solx.at[1], dsend.at[5], drecv.at[5], has_s)
        for n in range(4):
            x = jnp.zeros((16, 128), F32)
            for r in range(NG):
                x = jnp.where(lane16 == r, roll(ewr[r], r - n, 1), x)
            wst[n] = x
        for n, ref in ((4, dpx.at[0]), (5, solx.at[0])):
            x = jnp.zeros((16, 128), F32)
            for r in range(NG):
                row = jnp.broadcast_to(ref[r : r + 1, :].astype(F32), (16, 128))
                x = jnp.where(lane16 == r, roll(row, r + 1, 1), x)
            wst[n] = x

    def await_light():
        for k, g in enumerate(peers):
            arrived(pall.at[g], psend.at[1, k], precv.at[1, g])
        for g in range(NG):
            arrived(psr.at[g], xsend.at[0, g], xrecv.at[0, g], has_s)
            arrived(pwr.at[g], xsend.at[1, g], xrecv.at[1, g], has_w)

    def window(state, edge, n):
        return jnp.concatenate([state, edges(edge[2 * n : 2 * n + 1, :], edge[2 * n + 1 : 2 * n + 2, :])], axis=0)

    level16 = (jnp.where(row16 <= 8, row16, -1) + 8 * b).astype(F32)
    has_above = jnp.logical_or(row16 <= 8, b > 0)

    def band_ocean(pigment, surface, depth, temp, sal, quiet, movers):
        att_of = lambda x: 0.01 + 0.05 * x
        prefix = jnp.zeros((8, 128), F32)
        for g in range(NG):
            x = att_of(pigment(g))
            for s in (4, 2, 1):
                x = x + roll(x, s, 0)
            prefix = prefix + jnp.where(g < b, x, 0.0)
        own = att_of(pigment(b))
        att_hi = att_of(pigment(jnp.minimum(b + 1, NG - 1))[0:1])
        att_lo = att_of(pigment(jnp.maximum(b - 1, 0))[7:8])
        cum = own
        for s in (1, 2, 4):
            cum = cum + jnp.where(row8 >= s, roll(cum, s, 0), 0.0)
        att = jnp.concatenate([own, edges(att_hi, att_lo)], axis=0)
        above = jnp.concatenate([prefix + (cum - own), prefix + edges(cum[7:8], -att_lo)], axis=0)
        wet = jnp.where(level16 < depth, 1.0, 0.0)
        top = surface * jnp.exp(-above)
        temp = temp + 5.0 * (top * (1.0 - jnp.exp(-att))) * wet
        rho = 0.8 * sal - 0.2 * temp
        strat = roll(rho, 15, 0) - rho
        face = (0.5 * (quiet + roll(quiet, 15, 0)) + 0.15 * jax.nn.sigmoid(-strat)) * roll(wet, 15, 0)
        face = jnp.where(has_above, face, 0.0)

        def stir(x):
            flux = face * (roll(x, 15, 0) - x)
            return (x + flux - roll(flux, 1, 0))[0:8]

        par = top[0:8] * jnp.exp(-0.5 * own)
        return [stir(x) for x in movers] + [stir(temp), face[0:8], roll(face, 1, 0)[0:8], par]

    def forcing(t):
        if t == 0:
            got = [[fr[r, n] for n in range(NF)] for r in range(NG)]
            west = [ewr[r, 0:8] for r in range(NG)]
            south = vsr[...]
        else:
            wide = lambda x: jnp.broadcast_to(x.astype(F32), (16, 128))
            got = []
            for r in range(NG):
                u, v, temp = (window(fr[r, n], fr2[r, 1], n) for n in range(3))
                sal = window(fr2[r, 0], fr2[r, 1], 3)
                got.append(band_ocean(lambda g: pall[g, r], wide(sol[r : r + 1, :]), wide(dep[r : r + 1, :]), temp, sal, fqr[r], (u, v)))
            edge = n2r[3]
            v = window(vsr[...], edge, 0)
            temp, sal, quiet = (window(n2r[n], edge, n + 1) for n in range(3))
            south = band_ocean(lambda g: psr[g], wide(solx[1, NG - 1 : NG, :]), wide(dpx[2, NG - 1 : NG, :]), temp, sal, quiet, (v,))[0]
            uw = band_ocean(lambda g: pwr[g], wst[5], wst[4], wst[1], wst[2], wst[3], (wst[0],))[0]
            west = [roll(uw, -r, 1) if r else uw for r in range(NG)]
        return got, west, south

    def openings():
        for k in range(4):
            arrived(dpx.at[k], dsend.at[k], drecv.at[k], sides[k][0])
        level = (lax.broadcasted_iota(jnp.int32, (8, 128), 0) + 8 * b).astype(F32)

        def wet_of(rows):
            return jnp.where(level < jnp.broadcast_to(rows, (8, 128)), 1.0, 0.0)

        def row(ref, r):
            return jnp.broadcast_to(ref[r : r + 1, :].astype(F32), (8, 128))

        own = [row(dep, r) for r in range(NG)]
        wets = [wet_of(x) for x in own]
        wet_n = wet_of(row(dpx.at[3], 0))
        wet_s = wet_of(row(dpx.at[2], NG - 1))
        for r in range(NG):
            wet_e = jnp.where(lane8 == 127, roll(wet_of(row(dpx.at[1], r)), 127, 1), roll(wets[r], 127, 1))
            wet_w = jnp.where(lane8 == 0, roll(wet_of(row(dpx.at[0], r)), 1, 1), roll(wets[r], 1, 1))
            ops[0, r] = wets[r] * wet_e
            ops[1, r] = wets[r] * wet_w
            ops[2, r] = wets[r] * (wets[r + 1] if r < NG - 1 else wet_n)
            ops[3, r] = wets[r] * (wets[r - 1] if r > 0 else wet_s)
            ops[4, r] = 0.5 * wets[r]

    def halos(t):
        arrived(hs.at[t], hsend.at[t, 0], hrecv.at[t, 0], has_s)
        arrived(hn.at[t], hsend.at[t, 1], hrecv.at[t, 1], has_n)
        arrived(xw_r.at[t], hsend.at[t, 2], hrecv.at[t, 2], has_w)
        arrived(xe_r.at[t], hsend.at[t, 3], hrecv.at[t, 3], has_e)
        pw = xw_r[t]
        pe = xe_r[t]
        for i in range(NT):
            cw[i] = jnp.where(lane32 == 0, roll(pw, 128 - i, 1) if i else pw, cw[i])
            ce[i] = jnp.where(lane32 == 127, roll(pe, 127 - i, 1), ce[i])

        @pl.when(b > 0)
        def _():
            arrived(zup_r.at[t], hsend.at[t, 4], hrecv.at[t, 4])
            for i in range(NT):
                cu[i, pl.ds(0, NG, stride=8), :] = zup_r[t, i]

        @pl.when(b < NG - 1)
        def _():
            arrived(zdn_r.at[t], hsend.at[t, 5], hrecv.at[t, 5])
            for i in range(NT):
                cd[i, pl.ds(7, NG, stride=8), :] = zdn_r[t, i]

    def update(t):
        got, west, south = forcing(t)
        for r in range(NG):
            u, v, temp, d, dm, par = got[r]
            warm = jnp.exp(0.0633 * (temp - 20.0))
            uwest = jnp.where(lane8 == 0, west[r], roll(u, 1, 1))
            vsouth = got[r - 1][1] if r > 0 else south
            a_e = ops[0, r] * (jnp.maximum(u, 0.0) + 0.05)
            b_e = ops[0, r] * (0.05 - jnp.minimum(u, 0.0))
            a_w = ops[1, r] * (jnp.maximum(uwest, 0.0) + 0.05)
            b_w = ops[1, r] * (0.05 - jnp.minimum(uwest, 0.0))
            a_n = ops[2, r] * (jnp.maximum(v, 0.0) + 0.05)
            b_n = ops[2, r] * (0.05 - jnp.minimum(v, 0.0))
            a_s_ = ops[3, r] * (jnp.maximum(vsouth, 0.0) + 0.05)
            b_s = ops[3, r] * (0.05 - jnp.minimum(vsouth, 0.0))
            k0 = 1.0 - a_e - b_w - a_n - b_s - d - dm
            half = ops[4, r]
            warm = half * warm
            parw = half * par
            rows = pl.ds(8 * r, 8)

            def one(i, _):
                x = cs[t, i, rows, :]
                up = cs[t, i, pl.ds(8 * r + 8, 8), :] if r < NG - 1 else hn[t, i]
                dn = cs[t, i, pl.ds(8 * r - 8, 8), :] if r > 0 else hs[t, i]
                grow = k0 + ph_s[i] * parw / (par + sat_s[i])
                new = (
                    grow * x
                    + (b_e * ce[i, rows, :] + a_w * cw[i, rows, :])
                    + (b_n * up + a_s_ * dn)
                    + (d * cd[i, rows, :] + dm * cu[i, rows, :])
                    + warm * mix[i, rows, :]
                )
                if t == STEPS - 1:
                    oc[pl.ds(i * 32 + r, 8, stride=4), :] = new
                else:
                    cs[t + 1, i, rows, :] = new
                return 0

            lax.fori_loop(0, NT, one, 0, unroll=True)

    loads[0].wait()
    for i in range(NT):
        for r in range(NG):
            cs[0, i, pl.ds(8 * r, 8), :] = cin[pl.ds(i * 32 + r, 8, stride=4), :]
    loads[8].wait()
    publish(0)
    for copy in loads[1:8] + loads[9:]:
        copy.wait()
    share_mixing()
    local_terms(0)
    openings()
    columns(0)
    share_state()
    halos(0)
    for k, g in enumerate(peers):
        arrived(fr.at[g], fsend.at[0, k], frecv.at[0, g])
    for g in range(NG):
        arrived(ewr.at[g], esend.at[g], erecv.at[g], has_w)
    arrived(vsr, nsend.at[0, 0], nrecv.at[0], has_s)
    update(0)
    publish(1)
    local_terms(1)
    await_state()
    halos(1)
    await_light()
    update(1)
    columns(1)

    for there, copy in sends:
        if there is None:
            copy.wait_send()
        else:
            pl.when(there)(copy.wait_send)


def write_out(*refs):
    n = (len(refs) - 1) // 2
    copies = [pltpu.make_async_copy(refs[k], refs[n + k], refs[-1].at[k]) for k in range(n)]
    for copy in copies:
        copy.start()
    for copy in copies:
        copy.wait()


def per_device(nx, ny, *args):
    u, v, temp, sal, quiet, c, dep, sol, rates, photo, satur, pig = args
    shape = u.shape
    fields = [x.reshape(32, 128) for x in (u, v, temp, sal, quiet)]
    hbm = pl.BlockSpec(memory_space=pltpu.HBM)
    vmem = pl.BlockSpec(memory_space=pltpu.VMEM)
    col = jax.ShapeDtypeStruct((32, 128), F32)
    V = pltpu.VMEM
    D = pltpu.SemaphoreType.DMA
    S = STEPS
    out = pl.pallas_call(
        functools.partial(kernel, nx, ny),
        out_shape=(col, col, col, col, jax.ShapeDtypeStruct((NT * 32, 128), F32)),
        in_specs=[hbm] * 12,
        out_specs=(vmem,) * 5,
        scratch_shapes=[
            pltpu.SMEM((NT, NT), F32), pltpu.SMEM((NT,), F32), pltpu.SMEM((NT,), F32), pltpu.SMEM((NT,), F32),
            V((NT * 32, 128), F32), V((5, 32, 128), F32), V((4, 128), jnp.int32), V((4, 128), F32),
            V((S, NT, 32, 128), F32), V((S, NT, 8, 128), F32), V((S, NT, 8, 128), F32),
            V((S, NT, 4, 128), F32), V((S, NT, 4, 128), F32), V((S, NT, 4, 128), F32), V((S, NT, 4, 128), F32),
            V((S, 32, 128), F32), V((S, 32, 128), F32), V((S, 32, 128), F32), V((S, 32, 128), F32),
            V((S, NG, 8, 128), F32), V((32, 128), F32),
            V((NG, NF, 8, 128), F32), V((NG, NF, 8, 128), F32),
            V((32, 128), F32), V((8, 128), F32),
            V((4, 4, 128), jnp.int32), V((5, NG, 8, 128), F32),
            V((NT, 32, 128), F32), V((NT, 32, 128), F32), V((NT, 32, 128), F32), V((NT, 32, 128), F32), V((NT, 32, 128), F32),
            V((NG, NG, 8, 128), F32), V((8, 128), F32), V((NG, 8, 128), F32), V((NG, 8, 128), F32),
            V((NG, 2, 8, 128), F32), V((NG, 2, 8, 128), F32), V((NG, 16, 128), F32), V((NG, 16, 128), F32),
            V((32, 128), F32), V((NG, 16, 128), F32), V((NG, 16, 128), F32),
            V((NG, 4, 8, 128), F32), V((4, 8, 128), F32), V((2, 4, 128), F32), V((6, 16, 128), F32),
            D((12,)), D((S, 3)), D((S, NG)), D((S, 3)), D((S, NG)), D((NG,)), D((NG,)), D((S, NG)), D((S,)),
            D((S, 6)), D((S, 6)), D((6,)), D((6,)), D((3, NG)), D((3, NG)),
        ],
        compiler_params=pltpu.CompilerParams(collective_id=0, has_side_effects=True, vmem_limit_bytes=16 << 20),
    )(*[pltpu.with_memory_space_constraint(x, pltpu.HBM) for x in (*fields, c.reshape(NT * 32, 128), dep, sol, rates, photo, satur, pig)])
    out = pl.pallas_call(
        write_out,
        out_shape=(col, col, col, col, jax.ShapeDtypeStruct((NT * 32, 128), F32)),
        in_specs=[vmem] * 5,
        out_specs=(hbm,) * 5,
        scratch_shapes=[D((5,))],
        compiler_params=pltpu.CompilerParams(vmem_limit_bytes=4 << 20),
    )(*out)
    return tuple(x.reshape(shape) for x in out[:4]) + (out[4].reshape(c.shape),)


def solution(mesh):
    field = P(None, "gy", "grp", "gx")
    tracer = P(None, "grp", "gy", "gx")
    flat = P("gy", "gx")
    return jax.shard_map(
        functools.partial(per_device, mesh.shape["gx"], mesh.shape["gy"]),
        mesh=mesh,
        in_specs=(field,) * 5 + (tracer, flat, flat, P(), P(), P(), P()),
        out_specs=(field,) * 4 + (tracer,),
        check_vma=False,
    )
```

```python
import functools

import jax
import jax.numpy as jnp
from jax import lax
from jax.experimental import pallas as pl
from jax.experimental.pallas import tpu as pltpu
from jax.sharding import PartitionSpec as P

STEPS = 2
NG = 4
NT = 19
F32 = jnp.float32
NF = 3
SEND = ("pig", "dep0", "dep1", "dep2", "dep3", "solw", "sols", "h0", "h1", "h2", "h3", "h4", "h5", "fixed", "force", "edge", "state", "v", "row", "u", "col", "sums", "ssum", "wsum", "span", "wpan", "cols")
RECV = SEND[:7] + tuple(f"h{n}{t}" for n in range(6) for t in range(2)) + SEND[13:]


def roll(x, shift, axis):
    return pltpu.roll(x, shift % x.shape[axis], axis)


def kernel(
    nx, ny,
    u_hbm, v_hbm, t_hbm, s_hbm, q_hbm, c_hbm, dep_hbm, sol_hbm, a_hbm, ph_hbm, sat_hbm, pig_hbm,
    ou, ov, ot, osl, oc,
    a_s, ph_s, sat_s, pig_s, cin, oc_in, dep, sol, cs, hs, hn, zup_s, zdn_s, zup_r, zdn_r, xe_s, xw_s, xe_r, xw_r,
    ps, pf, fs, fr, vsh, vsr, dpx, ops, mix, cw, ce, cu, cd,
    uv, dls, dlr, pcs, pcr, scs, scr, wcs, wcr, pws, pwr, psr, fs2, fr2, fqs, fqr, ep, ews, ewr, ewx, n2s, n2r, solx, wst,
    loc, ssems, rsems,
):
    b = lax.axis_index("grp")
    ix = lax.axis_index("gx")
    iy = lax.axis_index("gy")
    has_e, has_w, has_n, has_s = ix < nx - 1, ix > 0, iy < ny - 1, iy > 0
    east, west, north, south = {"gx": ix + 1}, {"gx": ix - 1}, {"gy": iy + 1}, {"gy": iy - 1}
    sides = ((has_w, west), (has_e, east), (has_s, south), (has_n, north))
    peers = [lax.rem(b + k, NG) for k in (2, 3, 1)]

    loads = [pltpu.make_async_copy(c_hbm, cin, loc.at[0])]
    for n, (ref, dst) in enumerate(((pig_hbm, pig_s), (dep_hbm, dep), (sol_hbm, sol), (a_hbm, a_s), (ph_hbm, ph_s), (sat_hbm, sat_s))):
        loads.append(pltpu.make_async_copy(ref, dst, loc.at[1 + n]))
    for n, ref in enumerate((u_hbm, v_hbm, t_hbm, s_hbm, q_hbm)):
        loads.append(pltpu.make_async_copy(ref, oc_in.at[n], loc.at[7]))
    for copy in loads:
        copy.start()

    barrier = pltpu.get_barrier_semaphore()
    for g in peers:
        pl.semaphore_signal(barrier, inc=1, device_id={"grp": g})
    for there, dev in sides[::-1]:

        @pl.when(there)
        def _():
            for g in range(NG):
                pl.semaphore_signal(barrier, inc=1, device_id={"grp": g, **dev})

    lane8 = lax.broadcasted_iota(jnp.int32, (8, 128), 1)
    lane32 = lax.broadcasted_iota(jnp.int32, (32, 128), 1)
    row8 = lax.broadcasted_iota(jnp.int32, (8, 128), 0)
    row16 = lax.broadcasted_iota(jnp.int32, (16, 128), 0)
    lane16 = lax.broadcasted_iota(jnp.int32, (16, 128), 1)
    row32 = lax.broadcasted_iota(jnp.int32, (32, 128), 0)
    pending = []

    def remote(src, dst, name, dev):
        tag, at = (name[:2], name) if name[0] == "h" else (name, name)
        return pltpu.make_async_remote_copy(src, dst, ssems.at[SEND.index(tag)], rsems.at[RECV.index(at)], device_id=dev, device_id_type=pl.DeviceIdType.MESH)

    def guarded(there, act):
        if there is None:
            act()
        else:
            pl.when(there)(act)

    def send(src, dst, name, dev, there=None, whole=None):
        if whole is not False:
            pending.append((there, src if whole is None else whole, name))
        guarded(there, remote(src, dst, name, dev).start)

    def sent(names=None):
        for there, ref, name in pending:
            if names is None or name in names:
                guarded(there, remote(ref, ref, name, {"grp": peers[0]}).wait_send)
        pending[:] = [x for x in pending if names is not None and x[2] not in names]

    def arrived(ref, name, there=None):
        guarded(there, remote(ref, ref, name, {"grp": peers[0]}).wait_recv)

    def first(k, ref):
        return ref if k == 0 else False

    for there, refs in ((has_w, (ewr, ewx, xw_r, pwr, wcr, solx.at[0])), (has_e, (xe_r,)), (has_s, (vsr, hs, n2r, psr, scr, solx.at[1])), (has_n, (hn,))):

        @pl.when(jnp.logical_not(there))
        def _():
            for ref in refs:
                ref[...] = jnp.zeros_like(ref)

    for k, (there, _) in enumerate(sides):

        @pl.when(jnp.logical_not(there))
        def _():
            dpx[k] = jnp.zeros((4, 128), jnp.int32)

    def publish(t):
        pig = jnp.zeros((32, 128), F32)
        for i in range(NT):
            pig = pig + pig_s[i] * cs[t, i]
        for r in range(NG):
            ps[t, r] = pig[8 * r : 8 * r + 8]
        pf[t, pl.ds(pl.multiple_of(b * 8, 8), 8), :] = ps[t, b]
        mine = pf.at[t, pl.ds(pl.multiple_of(b * 8, 8), 8), :]
        if t == 0:
            pl.semaphore_wait(barrier, NG - 1 + NG * sum(there.astype(jnp.int32) for there, _ in sides))
            for k, g in enumerate(peers):
                send(ps.at[t, g], mine, "pig", {"grp": g}, whole=first(k, ps.at[t, 0:3]))
        else:
            def total(x):
                for n in (4, 2, 1):
                    x = x + roll(x, n, 0)
                return x[0:1]

            for r in range(NG):
                x = 0.01 + 0.05 * ps[t, r]
                whole = total(x)
                for n, edge in enumerate((x[7:8], x[0:1])):
                    pcs[n, r : r + 1] = whole
                    pcs[n, NG + r : NG + r + 1] = edge
            pack = jnp.zeros((8, 128), F32)
            for r in range(NG):
                pack = jnp.where(lane8 == r, roll(ps[t, r], r + 1, 1), pack)
            pws[...] = pack
            for ref, x in ((scs, ps[t, NG - 1]), (wcs, pack)):
                x = 0.01 + 0.05 * x
                whole = total(x)
                for n, edge in enumerate((x[7:8], x[0:1])):
                    ref[n, 0:1] = whole
                    ref[n, 1:2] = edge
            for k, g in enumerate(peers):
                send(pcs.at[(g < b).astype(jnp.int32)], pcr.at[b], "sums", {"grp": g}, whole=first(k, pcr.at[0:3]))
            for k, g in enumerate(peers):
                side = (g < b).astype(jnp.int32)
                send(scs.at[side], scr.at[b], "ssum", {"grp": g, **north}, has_n, first(k, scr.at[0:3]))
                send(wcs.at[side], wcr.at[b], "wsum", {"grp": g, **east}, has_e, first(k, wcr.at[0:3]))
            send(ps.at[t, NG - 1], psr, "span", north, has_n)
            send(pws, pwr, "wpan", east, has_e)
            pcr[b] = pcs[0]
            scr[b] = scs[0]
            wcr[b] = wcs[0]
        if t == 0:
            for k, (there, dev) in enumerate(sides):
                send(dep_hbm, dpx.at[k ^ 1], f"dep{k ^ 1}", dev, there)
            send(sol_hbm, solx.at[0], "solw", east, has_e)
            send(sol_hbm, solx.at[1], "sols", north, has_n)
        if t == 1:
            sent([f"h{n}0" for n in range(6)])
        send(cs.at[t, :, pl.ds(24, 8), :], hs.at[t], f"h0{t}", north, has_n)
        send(cs.at[t, :, pl.ds(0, 8), :], hn.at[t], f"h1{t}", south, has_s)
        pe = jnp.zeros((32, 128), F32)
        pw = jnp.zeros((32, 128), F32)
        for i in range(NT):
            x = cs[t, i]
            pe = jnp.where(lane32 == i, roll(x, i + 1, 1), pe)
            pw = jnp.where(lane32 == i, roll(x, i, 1) if i else x, pw)
        xe_s[t] = pe
        xw_s[t] = pw
        send(xe_s.at[t], xw_r.at[t], f"h2{t}", east, has_e)
        send(xw_s.at[t], xe_r.at[t], f"h3{t}", west, has_w)
        for i in range(NT):
            zup_s[t, i] = cs[t, i, pl.ds(7, NG, stride=8), :]
            zdn_s[t, i] = cs[t, i, pl.ds(0, NG, stride=8), :]

        send(zup_s.at[t], zup_r.at[t], f"h4{t}", {"grp": b + 1}, b < NG - 1)
        send(zdn_s.at[t], zdn_r.at[t], f"h5{t}", {"grp": b - 1}, b > 0)
        if t == 1:
            for k, g in enumerate(peers):
                send(ps.at[t, g], mine, "cols", {"grp": g}, whole=first(k, ps.at[t, 0:3]))

    def local_terms(t):
        def mixing(i, _):
            acc = a_s[i, 0] * cs[t, 0]
            for j in range(1, NT):
                acc = acc + a_s[i, j] * cs[t, j]
            mix[i] = acc
            x = cs[t, i]
            cw[i] = roll(x, 1, 1)
            ce[i] = roll(x, 127, 1)
            cu[i] = roll(x, 1, 0)
            cd[i] = roll(x, 31, 0)
            return 0

        lax.fori_loop(0, NT, mixing, 0)

    def bound(x):
        return min(max(x, 0), 31)

    def edges(hi, lo):
        return jnp.where(row8 == 0, jnp.broadcast_to(hi, (8, 128)), jnp.broadcast_to(lo, (8, 128)))

    def share_fixed():
        for g in range(NG):
            hi, lo = bound(8 * g + 8), bound(8 * g - 1)
            for n, x in enumerate((0, 1, 4)):
                fqs[g, n] = oc_in[x, 8 * g : 8 * g + 8]
            for n, x in enumerate((0, 1, 4, 4)):
                fqs[g, 3, 2 * n : 2 * n + 1] = oc_in[x, hi : hi + 1]
                fqs[g, 3, 2 * n + 1 : 2 * n + 2] = oc_in[x, lo : lo + 1]
        for k, g in enumerate(peers):
            send(fqs.at[g], fqr.at[b], "fixed", {"grp": g}, whole=first(k, fqs.at[0:3]))
        fqr[b] = fqs[b]

    def columns(t):
        if t == 0:
            arrived(pf.at[t, 0:24], "pig")
            u, v, temp, sal = (oc_in[n] for n in range(4))
        else:
            u, v, temp, sal = ou[...], ov[...], ot[...], osl[...]
        att = 0.01 + 0.05 * pf[t]
        cum = att
        for s in (1, 2, 4, 8, 16):
            cum = cum + jnp.where(row32 >= s, roll(cum, s, 0), 0.0)
        top = sol[pl.ds(b, 1), :] * jnp.exp(att - cum)
        heating = top * (1.0 - jnp.exp(-att))
        wet = (row32 < dep[pl.ds(b, 1), :]).astype(F32)
        quiet = oc_in[4]
        temp = temp + 5.0 * heating * wet
        rho = 0.8 * sal - 0.2 * temp
        strat = roll(rho, 31, 0) - rho
        face = (0.5 * (quiet + roll(quiet, 31, 0)) + 0.15 * jax.nn.sigmoid(-strat)) * roll(wet, 31, 0)
        face = jnp.where(row32 < 31, face, 0.0)

        def stir(x):
            flux = face * (roll(x, 31, 0) - x)
            return x + flux - roll(flux, 1, 0)

        u, v, temp, sal = stir(u), stir(v), stir(temp), stir(sal)
        if t == 0:
            par = top * jnp.exp(-0.5 * att)
            for n, x in enumerate((temp, face, par)):
                for g in range(NG):
                    fs[g, n] = x[8 * g : 8 * g + 8]
            dls[0] = jnp.zeros((1, 128), F32)
            for g in range(1, NG):
                dls[g] = face[8 * g - 1 : 8 * g]
            for k, g in enumerate(peers):
                send(fs.at[g], fr.at[b], "force", {"grp": g}, whole=first(k, fs.at[0:3]))
                send(dls.at[g], dlr.at[b], "edge", {"grp": g}, whole=first(k, dls.at[0:3]))
            vsh[...] = v
            for g in range(NG):
                send(vsh.at[pl.ds(8 * g, 8), :], vsr, "v", {"grp": g, **north}, jnp.logical_and(b == NG - 1, has_n), first(g, vsh))
            pack = jnp.zeros((32, 128), F32)
            for n, x in enumerate((u, temp, sal, quiet)):
                pack = jnp.where(lane32 == n, roll(x, n + 1, 1), pack)
            ep[...] = pack
            for g in range(NG):
                send(ep.at[8 * g : 8 * g + 8], ewr.at[b], "u", {"grp": g, **east}, has_e, first(g, ep))
            fr[b] = fs[b]
            dlr[b] = dls[b]
        ou[...] = u
        ov[...] = v
        ot[...] = temp
        osl[...] = sal

    def share_state():
        for g in range(NG):
            hi, lo = bound(8 * g + 8), bound(8 * g - 1)
            fs2[g, 0] = osl[8 * g : 8 * g + 8]
            for n, x in enumerate((ou, ov, ot, osl)):
                fs2[g, 1, 2 * n : 2 * n + 1] = x[hi : hi + 1]
                fs2[g, 1, 2 * n + 1 : 2 * n + 2] = x[lo : lo + 1]
        for k, g in enumerate(peers):
            send(fs2.at[g], fr2.at[b], "state", {"grp": g}, whole=first(k, fs2.at[0:3]))
        fr2[b] = fs2[b]
        for g in range(NG):
            hi, lo = bound(8 * g + 8), bound(8 * g - 1)
            ews[g] = edges(ep[hi : hi + 1], ep[lo : lo + 1])
            send(ews.at[g], ewx.at[b], "col", {"grp": g, **east}, has_e, first(g, ews))
        quiet = oc_in.at[4]
        for g in range(NG):
            hi, lo = bound(8 * g + 8), bound(8 * g - 1)
            for n, x in enumerate((ot, osl, quiet)):
                n2s[g, n] = x[8 * g : 8 * g + 8]
            for n, x in enumerate((ov, ot, osl, quiet)):
                n2s[g, 3, 2 * n : 2 * n + 1] = x[hi : hi + 1]
                n2s[g, 3, 2 * n + 1 : 2 * n + 2] = x[lo : lo + 1]
            send(n2s.at[g], n2r, "row", {"grp": g, **north}, jnp.logical_and(b == NG - 1, has_n), first(g, n2s))

    def await_state():
        arrived(fr2.at[0:3], "state")
        arrived(ewx, "col", has_w)
        arrived(n2r, "row", has_s)
        arrived(solx.at[0], "solw", has_w)
        arrived(solx.at[1], "sols", has_s)
        for n in range(4):
            x = jnp.zeros((16, 128), F32)
            for r in range(NG):
                x = jnp.where(lane16 == r, roll(jnp.concatenate([ewr[r], ewx[r]], axis=0), r - n, 1), x)
            wst[n] = x
        for n, ref in ((4, dpx.at[0]), (5, solx.at[0])):
            x = jnp.zeros((16, 128), F32)
            for r in range(NG):
                row = jnp.broadcast_to(ref[r : r + 1, :].astype(F32), (16, 128))
                x = jnp.where(lane16 == r, roll(row, r + 1, 1), x)
            wst[n] = x

    def await_light():
        arrived(pcr.at[0:3], "sums")
        arrived(scr.at[0:3], "ssum", has_s)
        arrived(wcr.at[0:3], "wsum", has_w)
        arrived(pf.at[1, 0:24], "cols")
        arrived(psr, "span", has_s)
        arrived(pwr, "wpan", has_w)

    def window(state, edge, n):
        return jnp.concatenate([state, edges(edge[2 * n : 2 * n + 1, :], edge[2 * n + 1 : 2 * n + 2, :])], axis=0)

    level16 = (jnp.where(row16 <= 8, row16, -1) + 8 * b).astype(F32)
    has_above = jnp.logical_or(row16 <= 8, b > 0)

    below, over = jnp.minimum(b + 1, NG - 1), jnp.maximum(b - 1, 0)

    def band_ocean(pigment, total, edge, surface, depth, temp, sal, quiet, movers):
        prefix = jnp.zeros((1, 128), F32)
        for g in range(NG):
            prefix = prefix + jnp.where(g < b, total(g), 0.0)
        prefix = jnp.broadcast_to(prefix, (8, 128))
        own = 0.01 + 0.05 * pigment
        att_hi, att_lo = edge(below), edge(over)
        cum = own
        for s in (1, 2, 4):
            cum = cum + jnp.where(row8 >= s, roll(cum, s, 0), 0.0)
        att = jnp.concatenate([own, edges(att_hi, att_lo)], axis=0)
        above = jnp.concatenate([prefix + (cum - own), prefix + edges(cum[7:8], -att_lo)], axis=0)
        wet = jnp.where(level16 < depth, 1.0, 0.0)
        top = surface * jnp.exp(-above)
        temp = temp + 5.0 * (top * (1.0 - jnp.exp(-att))) * wet
        rho = 0.8 * sal - 0.2 * temp
        strat = roll(rho, 15, 0) - rho
        face = (0.5 * (quiet + roll(quiet, 15, 0)) + 0.15 * jax.nn.sigmoid(-strat)) * roll(wet, 15, 0)
        face = jnp.where(has_above, face, 0.0)

        def stir(x):
            flux = face * (roll(x, 15, 0) - x)
            return (x + flux - roll(flux, 1, 0))[0:8]

        par = top[0:8] * jnp.exp(-0.5 * own)
        return [stir(x) for x in movers] + [stir(temp), face[0:8], roll(face, 1, 0)[0:8], par]

    def forcing(t):
        got = []
        if t == 0:
            for r in range(NG):
                temp, d, par = (fr[r, n] for n in range(NF))
                dm = jnp.where(row8 == 0, jnp.broadcast_to(dlr[r], (8, 128)), roll(d, 1, 0))
                moved = []
                for n in range(2):
                    x = fqr[r, n]
                    hi = jnp.broadcast_to(fqr[r, 3, 2 * n : 2 * n + 1], (8, 128))
                    lo = jnp.broadcast_to(fqr[r, 3, 2 * n + 1 : 2 * n + 2], (8, 128))
                    x = x + d * (jnp.where(row8 == 7, hi, roll(x, 7, 0)) - x) - dm * (x - jnp.where(row8 == 0, lo, roll(x, 1, 0)))
                    uv[r, n] = x
                    moved.append(x)
                got.append(moved + [temp, d, dm, par])
            west = [ewr[r] for r in range(NG)]
            south = vsr[...]
        else:
            wide = lambda x: jnp.broadcast_to(x.astype(F32), (16, 128))
            for r in range(NG):
                u, v = (window(uv[r, n], fr2[r, 1], n) for n in range(2))
                temp = window(fr[r, 0], fr2[r, 1], 2)
                sal = window(fr2[r, 0], fr2[r, 1], 3)
                quiet = window(fqr[r, 2], fqr[r, 3], 2)
                got.append(band_ocean(ps[1, r], lambda g: pcr[g, r : r + 1], lambda g: pcr[g, NG + r : NG + r + 1], wide(sol[r : r + 1, :]), wide(dep[r : r + 1, :]), temp, sal, quiet, (u, v)))
            edge = n2r[3]
            v = window(vsr[...], edge, 0)
            temp, sal, quiet = (window(n2r[n], edge, n + 1) for n in range(3))
            south = band_ocean(psr[...], lambda g: scr[g, 0:1], lambda g: scr[g, 1:2], wide(solx[1, NG - 1 : NG, :]), wide(dpx[2, NG - 1 : NG, :]), temp, sal, quiet, (v,))[0]
            uw = band_ocean(pwr[...], lambda g: wcr[g, 0:1], lambda g: wcr[g, 1:2], wst[5], wst[4], wst[1], wst[2], wst[3], (wst[0],))[0]
            west = [roll(uw, -r, 1) if r else uw for r in range(NG)]
        return got, west, south

    def openings():
        for k in range(4):
            arrived(dpx.at[k], f"dep{k}", sides[k][0])
        level = (lax.broadcasted_iota(jnp.int32, (8, 128), 0) + 8 * b).astype(F32)

        def wet_of(rows):
            return jnp.where(level < jnp.broadcast_to(rows, (8, 128)), 1.0, 0.0)

        def row(ref, r):
            return jnp.broadcast_to(ref[r : r + 1, :].astype(F32), (8, 128))

        own = [row(dep, r) for r in range(NG)]
        wets = [wet_of(x) for x in own]
        wet_n = wet_of(row(dpx.at[3], 0))
        wet_s = wet_of(row(dpx.at[2], NG - 1))
        for r in range(NG):
            wet_e = jnp.where(lane8 == 127, roll(wet_of(row(dpx.at[1], r)), 127, 1), roll(wets[r], 127, 1))
            wet_w = jnp.where(lane8 == 0, roll(wet_of(row(dpx.at[0], r)), 1, 1), roll(wets[r], 1, 1))
            ops[0, r] = wets[r] * wet_e
            ops[1, r] = wets[r] * wet_w
            ops[2, r] = wets[r] * (wets[r + 1] if r < NG - 1 else wet_n)
            ops[3, r] = wets[r] * (wets[r - 1] if r > 0 else wet_s)
            ops[4, r] = 0.5 * wets[r]

    def halos(t):
        arrived(hs.at[t], f"h0{t}", has_s)
        arrived(hn.at[t], f"h1{t}", has_n)
        arrived(xw_r.at[t], f"h2{t}", has_w)
        arrived(xe_r.at[t], f"h3{t}", has_e)
        pw = xw_r[t]
        pe = xe_r[t]
        for i in range(NT):
            cw[i] = jnp.where(lane32 == 0, roll(pw, 128 - i, 1) if i else pw, cw[i])
            ce[i] = jnp.where(lane32 == 127, roll(pe, 127 - i, 1), ce[i])

        @pl.when(b > 0)
        def _():
            arrived(zup_r.at[t], f"h4{t}")
            for i in range(NT):
                cu[i, pl.ds(0, NG, stride=8), :] = zup_r[t, i]

        @pl.when(b < NG - 1)
        def _():
            arrived(zdn_r.at[t], f"h5{t}")
            for i in range(NT):
                cd[i, pl.ds(7, NG, stride=8), :] = zdn_r[t, i]

    def update(t):
        got, west, south = forcing(t)
        for r in range(NG):
            u, v, temp, d, dm, par = got[r]
            warm = jnp.exp(0.0633 * (temp - 20.0))
            uwest = jnp.where(lane8 == 0, west[r], roll(u, 1, 1))
            vsouth = got[r - 1][1] if r > 0 else south
            a_e = ops[0, r] * (jnp.maximum(u, 0.0) + 0.05)
            b_e = ops[0, r] * (0.05 - jnp.minimum(u, 0.0))
            a_w = ops[1, r] * (jnp.maximum(uwest, 0.0) + 0.05)
            b_w = ops[1, r] * (0.05 - jnp.minimum(uwest, 0.0))
            a_n = ops[2, r] * (jnp.maximum(v, 0.0) + 0.05)
            b_n = ops[2, r] * (0.05 - jnp.minimum(v, 0.0))
            a_s_ = ops[3, r] * (jnp.maximum(vsouth, 0.0) + 0.05)
            b_s = ops[3, r] * (0.05 - jnp.minimum(vsouth, 0.0))
            k0 = 1.0 - a_e - b_w - a_n - b_s - d - dm
            half = ops[4, r]
            warm = half * warm
            parw = half * par
            rows = pl.ds(8 * r, 8)

            def one(i, _):
                x = cs[t, i, rows, :]
                up = cs[t, i, pl.ds(8 * r + 8, 8), :] if r < NG - 1 else hn[t, i]
                dn = cs[t, i, pl.ds(8 * r - 8, 8), :] if r > 0 else hs[t, i]
                grow = k0 + ph_s[i] * parw / (par + sat_s[i])
                new = (
                    grow * x
                    + (b_e * ce[i, rows, :] + a_w * cw[i, rows, :])
                    + (b_n * up + a_s_ * dn)
                    + (d * cd[i, rows, :] + dm * cu[i, rows, :])
                    + warm * mix[i, rows, :]
                )
                if t == STEPS - 1:
                    oc[pl.ds(i * 32 + r, 8, stride=4), :] = new
                else:
                    cs[t + 1, i, rows, :] = new
                return 0

            lax.fori_loop(0, NT, one, 0, unroll=True)

    loads[0].wait()
    for i in range(NT):
        for r in range(NG):
            cs[0, i, pl.ds(8 * r, 8), :] = cin[pl.ds(i * 32 + r, 8, stride=4), :]
    loads[1].wait()
    publish(0)
    for copy in loads[2:7] + [pltpu.make_async_copy(oc_in, oc_in, loc.at[7])]:
        copy.wait()
    share_fixed()
    local_terms(0)
    columns(0)
    share_state()
    openings()
    halos(0)
    arrived(fqr.at[0:3], "fixed")
    arrived(fr.at[0:3], "force")
    arrived(dlr.at[0:3], "edge")
    arrived(ewr, "u", has_w)
    arrived(vsr, "v", has_s)
    update(0)
    publish(1)
    local_terms(1)
    await_state()
    halos(1)
    await_light()
    update(1)
    columns(1)

    sent()


def write_out(*refs):
    n = (len(refs) - 1) // 2
    copies = [pltpu.make_async_copy(refs[k], refs[n + k], refs[-1].at[k]) for k in range(n)]
    for copy in copies:
        copy.start()
    for copy in copies:
        copy.wait()


def per_device(nx, ny, *args):
    u, v, temp, sal, quiet, c, dep, sol, rates, photo, satur, pig = args
    shape = u.shape
    fields = [x.reshape(32, 128) for x in (u, v, temp, sal, quiet)]
    hbm = pl.BlockSpec(memory_space=pltpu.HBM)
    vmem = pl.BlockSpec(memory_space=pltpu.VMEM)
    col = jax.ShapeDtypeStruct((32, 128), F32)
    V = pltpu.VMEM
    D = pltpu.SemaphoreType.DMA
    S = STEPS
    out = pl.pallas_call(
        functools.partial(kernel, nx, ny),
        out_shape=(col, col, col, col, jax.ShapeDtypeStruct((NT * 32, 128), F32)),
        in_specs=[hbm] * 12,
        out_specs=(vmem,) * 5,
        scratch_shapes=[
            pltpu.SMEM((NT, NT), F32), pltpu.SMEM((NT,), F32), pltpu.SMEM((NT,), F32), pltpu.SMEM((NT,), F32),
            V((NT * 32, 128), F32), V((5, 32, 128), F32), V((4, 128), jnp.int32), V((4, 128), F32),
            V((S, NT, 32, 128), F32), V((S, NT, 8, 128), F32), V((S, NT, 8, 128), F32),
            V((S, NT, 4, 128), F32), V((S, NT, 4, 128), F32), V((S, NT, 4, 128), F32), V((S, NT, 4, 128), F32),
            V((S, 32, 128), F32), V((S, 32, 128), F32), V((S, 32, 128), F32), V((S, 32, 128), F32),
            V((S, NG, 8, 128), F32), V((S, 32, 128), F32),
            V((NG, NF, 8, 128), F32), V((NG, NF, 8, 128), F32),
            V((32, 128), F32), V((8, 128), F32),
            V((4, 4, 128), jnp.int32), V((5, NG, 8, 128), F32),
            V((NT, 32, 128), F32), V((NT, 32, 128), F32), V((NT, 32, 128), F32), V((NT, 32, 128), F32), V((NT, 32, 128), F32),
            V((NG, 2, 8, 128), F32), V((NG, 1, 128), F32), V((NG, 1, 128), F32), V((2, 8, 128), F32), V((NG, 8, 128), F32),
            V((2, 2, 128), F32), V((NG, 2, 128), F32), V((2, 2, 128), F32), V((NG, 2, 128), F32),
            V((8, 128), F32), V((8, 128), F32), V((8, 128), F32),
            V((NG, 2, 8, 128), F32), V((NG, 2, 8, 128), F32), V((NG, 4, 8, 128), F32), V((NG, 4, 8, 128), F32),
            V((32, 128), F32), V((NG, 8, 128), F32), V((NG, 8, 128), F32), V((NG, 8, 128), F32),
            V((NG, 4, 8, 128), F32), V((4, 8, 128), F32), V((2, 4, 128), F32), V((6, 16, 128), F32),
            D((8,)), D((len(SEND),)), D((len(RECV),)),
        ],
        compiler_params=pltpu.CompilerParams(collective_id=0, has_side_effects=True, vmem_limit_bytes=16 << 20),
    )(*[pltpu.with_memory_space_constraint(x, pltpu.HBM) for x in (*fields, c.reshape(NT * 32, 128), dep, sol, rates, photo, satur, pig)])
    out = pl.pallas_call(
        write_out,
        out_shape=(col, col, col, col, jax.ShapeDtypeStruct((NT * 32, 128), F32)),
        in_specs=[vmem] * 5,
        out_specs=(hbm,) * 5,
        scratch_shapes=[D((5,))],
        compiler_params=pltpu.CompilerParams(vmem_limit_bytes=4 << 20),
    )(*out)
    return tuple(x.reshape(shape) for x in out[:4]) + (out[4].reshape(c.shape),)


def solution(mesh):
    field = P(None, "gy", "grp", "gx")
    tracer = P(None, "grp", "gy", "gx")
    flat = P("gy", "gx")
    return jax.shard_map(
        functools.partial(per_device, mesh.shape["gx"], mesh.shape["gy"]),
        mesh=mesh,
        in_specs=(field,) * 5 + (tracer, flat, flat, P(), P(), P(), P()),
        out_specs=(field,) * 4 + (tracer,),
        check_vma=False,
    )
```

```python
import functools

import jax
import jax.numpy as jnp
from jax import lax
from jax.experimental import pallas as pl
from jax.experimental.pallas import tpu as pltpu
from jax.sharding import PartitionSpec as P

STEPS = 2
NG = 4
NT = 19
F32 = jnp.float32
NF = 3
SEND = ("pig", "dep0", "dep1", "dep2", "dep3", "solw", "sols", "h0", "h1", "h2", "h3", "h4", "h5", "fixed", "force", "edge", "state", "v", "row", "u", "col", "sums", "ssum", "wsum", "span", "wpan", "cols")
RECV = SEND[:7] + tuple(f"h{n}{t}" for n in range(6) for t in range(2)) + SEND[13:]


def roll(x, shift, axis):
    return pltpu.roll(x, shift % x.shape[axis], axis)


def kernel(
    nx, ny,
    u_hbm, v_hbm, t_hbm, s_hbm, q_hbm, c_hbm, dep_hbm, sol_hbm, a_hbm, ph_hbm, sat_hbm, pig_hbm,
    ou, ov, ot, osl, oc,
    a_s, ph_s, sat_s, pig_s, cin, oc_in, dep, sol, cs, hs, hn, zup_s, zdn_s, zup_r, zdn_r, xe_s, xw_s, xe_r, xw_r,
    ps, pf, fs, fr, vsh, vsr, dpx, ops, mix, cw, ce, cu, cd,
    pst, psn, grown, kept, uv, dls, dlr, pcs, pcr, scs, scr, wcs, wcr, pws, pwr, psr, fs2, fr2, fqs, fqr, ep, ews, ewr, ewx, n2s, n2r, solx, wst,
    loc, ssems, rsems,
):
    b = lax.axis_index("grp")
    ix = lax.axis_index("gx")
    iy = lax.axis_index("gy")
    has_e, has_w, has_n, has_s = ix < nx - 1, ix > 0, iy < ny - 1, iy > 0
    east, west, north, south = {"gx": ix + 1}, {"gx": ix - 1}, {"gy": iy + 1}, {"gy": iy - 1}
    sides = ((has_w, west), (has_e, east), (has_s, south), (has_n, north))
    peers = [lax.rem(b + k, NG) for k in (2, 3, 1)]

    cuts = (0, 6, 13, NT)
    loads = []
    for n in range(3):
        part = pl.ds(32 * cuts[n], 32 * (cuts[n + 1] - cuts[n]))
        loads.append(pltpu.make_async_copy(c_hbm.at[part], cin.at[part], loc.at[(0, 8, 9)[n]]))
    for n, (ref, dst) in enumerate(((pig_hbm, pig_s), (dep_hbm, dep), (sol_hbm, sol), (a_hbm, a_s), (ph_hbm, ph_s), (sat_hbm, sat_s))):
        loads.append(pltpu.make_async_copy(ref, dst, loc.at[1 + n]))
    for n, ref in enumerate((u_hbm, v_hbm, t_hbm, s_hbm, q_hbm)):
        loads.append(pltpu.make_async_copy(ref, oc_in.at[n], loc.at[7]))
    for copy in loads:
        copy.start()

    barrier = pltpu.get_barrier_semaphore()
    for g in peers:
        pl.semaphore_signal(barrier, inc=1, device_id={"grp": g})
    for there, dev in sides[::-1]:

        @pl.when(there)
        def _():
            for g in range(NG):
                pl.semaphore_signal(barrier, inc=1, device_id={"grp": g, **dev})

    lane8 = lax.broadcasted_iota(jnp.int32, (8, 128), 1)
    lane32 = lax.broadcasted_iota(jnp.int32, (32, 128), 1)
    row8 = lax.broadcasted_iota(jnp.int32, (8, 128), 0)
    row16 = lax.broadcasted_iota(jnp.int32, (16, 128), 0)
    lane16 = lax.broadcasted_iota(jnp.int32, (16, 128), 1)
    row32 = lax.broadcasted_iota(jnp.int32, (32, 128), 0)
    pending = []

    def remote(src, dst, name, dev):
        tag, at = (name[:2], name) if name[0] == "h" else (name, name)
        return pltpu.make_async_remote_copy(src, dst, ssems.at[SEND.index(tag)], rsems.at[RECV.index(at)], device_id=dev, device_id_type=pl.DeviceIdType.MESH)

    def guarded(there, act):
        if there is None:
            act()
        else:
            pl.when(there)(act)

    def send(src, dst, name, dev, there=None, whole=None):
        if whole is not False:
            pending.append((there, src if whole is None else whole, name))
        guarded(there, remote(src, dst, name, dev).start)

    def sent(names=None):
        for there, ref, name in pending:
            if names is None or name in names:
                guarded(there, remote(ref, ref, name, {"grp": peers[0]}).wait_send)
        pending[:] = [x for x in pending if names is not None and x[2] not in names]

    def arrived(ref, name, there=None):
        guarded(there, remote(ref, ref, name, {"grp": peers[0]}).wait_recv)

    def first(k, ref):
        return ref if k == 0 else False

    for there, refs in ((has_w, (ewr, ewx, xw_r, pwr, wcr, solx.at[0])), (has_e, (xe_r,)), (has_s, (vsr, hs, n2r, psr, scr, solx.at[1])), (has_n, (hn,))):

        @pl.when(jnp.logical_not(there))
        def _():
            for ref in refs:
                ref[...] = jnp.zeros_like(ref)

    for k, (there, _) in enumerate(sides):

        @pl.when(jnp.logical_not(there))
        def _():
            dpx[k] = jnp.zeros((4, 128), jnp.int32)

    def publish_light(t):
        pf[t, pl.ds(pl.multiple_of(b * 8, 8), 8), :] = ps[t, b]
        mine = pf.at[t, pl.ds(pl.multiple_of(b * 8, 8), 8), :]
        if t == 0:
            pl.semaphore_wait(barrier, NG - 1 + NG * sum(there.astype(jnp.int32) for there, _ in sides))
            for k, g in enumerate(peers):
                send(ps.at[t, g], mine, "pig", {"grp": g}, whole=first(k, ps.at[t, 0:3]))
        else:
            def total(x):
                for n in (4, 2, 1):
                    x = x + roll(x, n, 0)
                return x[0:1]

            for r in range(NG):
                x = 0.01 + 0.05 * ps[t, r]
                whole = total(x)
                for n, edge in enumerate((x[7:8], x[0:1])):
                    pcs[n, r : r + 1] = whole
                    pcs[n, NG + r : NG + r + 1] = edge
            pack = jnp.zeros((8, 128), F32)
            for r in range(NG):
                pack = jnp.where(lane8 == r, roll(ps[t, r], r + 1, 1), pack)
            pws[...] = pack
            for ref, x in ((scs, ps[t, NG - 1]), (wcs, pack)):
                x = 0.01 + 0.05 * x
                whole = total(x)
                for n, edge in enumerate((x[7:8], x[0:1])):
                    ref[n, 0:1] = whole
                    ref[n, 1:2] = edge
            for k, g in enumerate(peers):
                send(pcs.at[(g < b).astype(jnp.int32)], pcr.at[b], "sums", {"grp": g}, whole=first(k, pcr.at[0:3]))
            for k, g in enumerate(peers):
                side = (g < b).astype(jnp.int32)
                send(scs.at[side], scr.at[b], "ssum", {"grp": g, **north}, has_n, first(k, scr.at[0:3]))
                send(wcs.at[side], wcr.at[b], "wsum", {"grp": g, **east}, has_e, first(k, wcr.at[0:3]))
            send(ps.at[t, NG - 1], psr, "span", north, has_n)
            send(pws, pwr, "wpan", east, has_e)
            pcr[b] = pcs[0]
            scr[b] = scs[0]
            wcr[b] = wcs[0]
        if t == 0:
            for k, (there, dev) in enumerate(sides):
                send(dep_hbm, dpx.at[k ^ 1], f"dep{k ^ 1}", dev, there)
            send(sol_hbm, solx.at[0], "solw", east, has_e)
            send(sol_hbm, solx.at[1], "sols", north, has_n)
    def publish_halos(t):
        mine = pf.at[t, pl.ds(pl.multiple_of(b * 8, 8), 8), :]
        if t == 1:
            for k, g in enumerate(peers):
                send(ps.at[t, g], mine, "cols", {"grp": g}, whole=first(k, ps.at[t, 0:3]))
            sent([f"h{n}0" for n in range(6)])
        send(cs.at[t, :, pl.ds(24, 8), :], hs.at[t], f"h0{t}", north, has_n)
        send(cs.at[t, :, pl.ds(0, 8), :], hn.at[t], f"h1{t}", south, has_s)
        pe = jnp.zeros((32, 128), F32)
        pw = jnp.zeros((32, 128), F32)
        for i in range(NT):
            x = cs[t, i]
            pe = jnp.where(lane32 == i, roll(x, i + 1, 1), pe)
            pw = jnp.where(lane32 == i, roll(x, i, 1) if i else x, pw)
        xe_s[t] = pe
        xw_s[t] = pw
        send(xe_s.at[t], xw_r.at[t], f"h2{t}", east, has_e)
        send(xw_s.at[t], xe_r.at[t], f"h3{t}", west, has_w)
        for i in range(NT):
            zup_s[t, i] = cs[t, i, pl.ds(7, NG, stride=8), :]
            zdn_s[t, i] = cs[t, i, pl.ds(0, NG, stride=8), :]

        send(zup_s.at[t], zup_r.at[t], f"h4{t}", {"grp": b + 1}, b < NG - 1)
        send(zdn_s.at[t], zdn_r.at[t], f"h5{t}", {"grp": b - 1}, b > 0)

    def local_terms(t):
        def mixing(i, _):
            acc = a_s[i, 0] * cs[t, 0]
            for j in range(1, NT):
                acc = acc + a_s[i, j] * cs[t, j]
            mix[i] = acc
            x = cs[t, i]
            cw[i] = roll(x, 1, 1)
            ce[i] = roll(x, 127, 1)
            cu[i] = roll(x, 1, 0)
            cd[i] = roll(x, 31, 0)
            return 0

        lax.fori_loop(0, NT, mixing, 0)

    def bound(x):
        return min(max(x, 0), 31)

    def edges(hi, lo):
        return jnp.where(row8 == 0, jnp.broadcast_to(hi, (8, 128)), jnp.broadcast_to(lo, (8, 128)))

    def share_fixed():
        for g in range(NG):
            hi, lo = bound(8 * g + 8), bound(8 * g - 1)
            for n, x in enumerate((0, 1, 4)):
                fqs[g, n] = oc_in[x, 8 * g : 8 * g + 8]
            for n, x in enumerate((0, 1, 4, 4)):
                fqs[g, 3, 2 * n : 2 * n + 1] = oc_in[x, hi : hi + 1]
                fqs[g, 3, 2 * n + 1 : 2 * n + 2] = oc_in[x, lo : lo + 1]
        for k, g in enumerate(peers):
            send(fqs.at[g], fqr.at[b], "fixed", {"grp": g}, whole=first(k, fqs.at[0:3]))
        fqr[b] = fqs[b]

    def columns(t):
        if t == 0:
            arrived(pf.at[t, 0:24], "pig")
            u, v, temp, sal = (oc_in[n] for n in range(4))
        else:
            u, v, temp, sal = ou[...], ov[...], ot[...], osl[...]
        att = 0.01 + 0.05 * pf[t]
        cum = att
        for s in (1, 2, 4, 8, 16):
            cum = cum + jnp.where(row32 >= s, roll(cum, s, 0), 0.0)
        top = sol[pl.ds(b, 1), :] * jnp.exp(att - cum)
        heating = top * (1.0 - jnp.exp(-att))
        wet = (row32 < dep[pl.ds(b, 1), :]).astype(F32)
        quiet = oc_in[4]
        temp = temp + 5.0 * heating * wet
        rho = 0.8 * sal - 0.2 * temp
        strat = roll(rho, 31, 0) - rho
        face = (0.5 * (quiet + roll(quiet, 31, 0)) + 0.15 * jax.nn.sigmoid(-strat)) * roll(wet, 31, 0)
        face = jnp.where(row32 < 31, face, 0.0)

        def stir(x):
            flux = face * (roll(x, 31, 0) - x)
            return x + flux - roll(flux, 1, 0)

        u, v, temp, sal = stir(u), stir(v), stir(temp), stir(sal)
        if t == 0:
            par = top * jnp.exp(-0.5 * att)
            for n, x in enumerate((temp, face, par)):
                for g in range(NG):
                    fs[g, n] = x[8 * g : 8 * g + 8]
            dls[0] = jnp.zeros((1, 128), F32)
            for g in range(1, NG):
                dls[g] = face[8 * g - 1 : 8 * g]
            for k, g in enumerate(peers):
                send(fs.at[g], fr.at[b], "force", {"grp": g}, whole=first(k, fs.at[0:3]))
                send(dls.at[g], dlr.at[b], "edge", {"grp": g}, whole=first(k, dls.at[0:3]))
            vsh[...] = v
            for g in range(NG):
                send(vsh.at[pl.ds(8 * g, 8), :], vsr, "v", {"grp": g, **north}, jnp.logical_and(b == NG - 1, has_n), first(g, vsh))
            pack = jnp.zeros((32, 128), F32)
            for n, x in enumerate((u, temp, sal, quiet)):
                pack = jnp.where(lane32 == n, roll(x, n + 1, 1), pack)
            ep[...] = pack
            for g in range(NG):
                send(ep.at[8 * g : 8 * g + 8], ewr.at[b], "u", {"grp": g, **east}, has_e, first(g, ep))
            fr[b] = fs[b]
            dlr[b] = dls[b]
        ou[...] = u
        ov[...] = v
        ot[...] = temp
        osl[...] = sal

    def share_state():
        for g in range(NG):
            hi, lo = bound(8 * g + 8), bound(8 * g - 1)
            fs2[g, 0] = osl[8 * g : 8 * g + 8]
            for n, x in enumerate((ou, ov, ot, osl)):
                fs2[g, 1, 2 * n : 2 * n + 1] = x[hi : hi + 1]
                fs2[g, 1, 2 * n + 1 : 2 * n + 2] = x[lo : lo + 1]
        for k, g in enumerate(peers):
            send(fs2.at[g], fr2.at[b], "state", {"grp": g}, whole=first(k, fs2.at[0:3]))
        fr2[b] = fs2[b]
        for g in range(NG):
            hi, lo = bound(8 * g + 8), bound(8 * g - 1)
            ews[g] = edges(ep[hi : hi + 1], ep[lo : lo + 1])
            send(ews.at[g], ewx.at[b], "col", {"grp": g, **east}, has_e, first(g, ews))
        quiet = oc_in.at[4]
        for g in range(NG):
            hi, lo = bound(8 * g + 8), bound(8 * g - 1)
            for n, x in enumerate((ot, osl, quiet)):
                n2s[g, n] = x[8 * g : 8 * g + 8]
            for n, x in enumerate((ov, ot, osl, quiet)):
                n2s[g, 3, 2 * n : 2 * n + 1] = x[hi : hi + 1]
                n2s[g, 3, 2 * n + 1 : 2 * n + 2] = x[lo : lo + 1]
            send(n2s.at[g], n2r, "row", {"grp": g, **north}, jnp.logical_and(b == NG - 1, has_n), first(g, n2s))

    def await_state():
        arrived(fr2.at[0:3], "state")
        arrived(ewx, "col", has_w)
        arrived(n2r, "row", has_s)
        arrived(solx.at[0], "solw", has_w)
        arrived(solx.at[1], "sols", has_s)
        for n in range(4):
            x = jnp.zeros((16, 128), F32)
            for r in range(NG):
                x = jnp.where(lane16 == r, roll(jnp.concatenate([ewr[r], ewx[r]], axis=0), r - n, 1), x)
            wst[n] = x
        for n, ref in ((4, dpx.at[0]), (5, solx.at[0])):
            x = jnp.zeros((16, 128), F32)
            for r in range(NG):
                row = jnp.broadcast_to(ref[r : r + 1, :].astype(F32), (16, 128))
                x = jnp.where(lane16 == r, roll(row, r + 1, 1), x)
            wst[n] = x

    def await_light():
        arrived(pcr.at[0:3], "sums")

    def await_sides():
        arrived(scr.at[0:3], "ssum", has_s)
        arrived(wcr.at[0:3], "wsum", has_w)
        arrived(psr, "span", has_s)
        arrived(pwr, "wpan", has_w)

    def window(state, edge, n):
        return jnp.concatenate([state, edges(edge[2 * n : 2 * n + 1, :], edge[2 * n + 1 : 2 * n + 2, :])], axis=0)

    level16 = (jnp.where(row16 <= 8, row16, -1) + 8 * b).astype(F32)
    has_above = jnp.logical_or(row16 <= 8, b > 0)

    below, over = jnp.minimum(b + 1, NG - 1), jnp.maximum(b - 1, 0)

    def band_ocean(pigment, total, edge, surface, depth, temp, sal, quiet, movers):
        prefix = jnp.zeros((1, 128), F32)
        for g in range(NG):
            prefix = prefix + jnp.where(g < b, total(g), 0.0)
        prefix = jnp.broadcast_to(prefix, (8, 128))
        own = 0.01 + 0.05 * pigment
        att_hi, att_lo = edge(below), edge(over)
        cum = own
        for s in (1, 2, 4):
            cum = cum + jnp.where(row8 >= s, roll(cum, s, 0), 0.0)
        att = jnp.concatenate([own, edges(att_hi, att_lo)], axis=0)
        above = jnp.concatenate([prefix + (cum - own), prefix + edges(cum[7:8], -att_lo)], axis=0)
        wet = jnp.where(level16 < depth, 1.0, 0.0)
        top = surface * jnp.exp(-above)
        temp = temp + 5.0 * (top * (1.0 - jnp.exp(-att))) * wet
        rho = 0.8 * sal - 0.2 * temp
        strat = roll(rho, 15, 0) - rho
        face = (0.5 * (quiet + roll(quiet, 15, 0)) + 0.15 * jax.nn.sigmoid(-strat)) * roll(wet, 15, 0)
        face = jnp.where(has_above, face, 0.0)

        def stir(x):
            flux = face * (roll(x, 15, 0) - x)
            return (x + flux - roll(flux, 1, 0))[0:8]

        par = top[0:8] * jnp.exp(-0.5 * own)
        return [stir(x) for x in movers] + [stir(temp), face[0:8], roll(face, 1, 0)[0:8], par]

    def forcing(t):
        got = []
        if t == 0:
            for r in range(NG):
                temp, d, par = (fr[r, n] for n in range(NF))
                dm = jnp.where(row8 == 0, jnp.broadcast_to(dlr[r], (8, 128)), roll(d, 1, 0))
                moved = []
                for n in range(2):
                    x = fqr[r, n]
                    hi = jnp.broadcast_to(fqr[r, 3, 2 * n : 2 * n + 1], (8, 128))
                    lo = jnp.broadcast_to(fqr[r, 3, 2 * n + 1 : 2 * n + 2], (8, 128))
                    x = x + d * (jnp.where(row8 == 7, hi, roll(x, 7, 0)) - x) - dm * (x - jnp.where(row8 == 0, lo, roll(x, 1, 0)))
                    uv[r, n] = x
                    moved.append(x)
                got.append(moved + [temp, d, dm, par])
            west = [ewr[r] for r in range(NG)]
            south = vsr[...]
        else:
            wide = lambda x: jnp.broadcast_to(x.astype(F32), (16, 128))
            for r in range(NG):
                u, v = (window(uv[r, n], fr2[r, 1], n) for n in range(2))
                temp = window(fr[r, 0], fr2[r, 1], 2)
                sal = window(fr2[r, 0], fr2[r, 1], 3)
                quiet = window(fqr[r, 2], fqr[r, 3], 2)
                got.append(band_ocean(ps[1, r], lambda g: pcr[g, r : r + 1], lambda g: pcr[g, NG + r : NG + r + 1], wide(sol[r : r + 1, :]), wide(dep[r : r + 1, :]), temp, sal, quiet, (u, v)))
            arrived(pf.at[1, 0:24], "cols")
            columns(1)
            await_sides()
            edge = n2r[3]
            v = window(vsr[...], edge, 0)
            temp, sal, quiet = (window(n2r[n], edge, n + 1) for n in range(3))
            south = band_ocean(psr[...], lambda g: scr[g, 0:1], lambda g: scr[g, 1:2], wide(solx[1, NG - 1 : NG, :]), wide(dpx[2, NG - 1 : NG, :]), temp, sal, quiet, (v,))[0]
            uw = band_ocean(pwr[...], lambda g: wcr[g, 0:1], lambda g: wcr[g, 1:2], wst[5], wst[4], wst[1], wst[2], wst[3], (wst[0],))[0]
            west = [roll(uw, -r, 1) if r else uw for r in range(NG)]
        return got, west, south

    def openings():
        for k in range(4):
            arrived(dpx.at[k], f"dep{k}", sides[k][0])
        level = (lax.broadcasted_iota(jnp.int32, (8, 128), 0) + 8 * b).astype(F32)

        def wet_of(rows):
            return jnp.where(level < jnp.broadcast_to(rows, (8, 128)), 1.0, 0.0)

        def row(ref, r):
            return jnp.broadcast_to(ref[r : r + 1, :].astype(F32), (8, 128))

        own = [row(dep, r) for r in range(NG)]
        wets = [wet_of(x) for x in own]
        wet_n = wet_of(row(dpx.at[3], 0))
        wet_s = wet_of(row(dpx.at[2], NG - 1))
        for r in range(NG):
            wet_e = jnp.where(lane8 == 127, roll(wet_of(row(dpx.at[1], r)), 127, 1), roll(wets[r], 127, 1))
            wet_w = jnp.where(lane8 == 0, roll(wet_of(row(dpx.at[0], r)), 1, 1), roll(wets[r], 1, 1))
            ops[0, r] = wets[r] * wet_e
            ops[1, r] = wets[r] * wet_w
            ops[2, r] = wets[r] * (wets[r + 1] if r < NG - 1 else wet_n)
            ops[3, r] = wets[r] * (wets[r - 1] if r > 0 else wet_s)
            ops[4, r] = 0.5 * wets[r]

    def halos(t):
        arrived(hs.at[t], f"h0{t}", has_s)
        arrived(hn.at[t], f"h1{t}", has_n)
        arrived(xw_r.at[t], f"h2{t}", has_w)
        arrived(xe_r.at[t], f"h3{t}", has_e)
        pw = xw_r[t]
        pe = xe_r[t]
        for i in range(NT):
            cw[i] = jnp.where(lane32 == 0, roll(pw, 128 - i, 1) if i else pw, cw[i])
            ce[i] = jnp.where(lane32 == 127, roll(pe, 127 - i, 1), ce[i])

        @pl.when(b > 0)
        def _():
            arrived(zup_r.at[t], f"h4{t}")
            for i in range(NT):
                cu[i, pl.ds(0, NG, stride=8), :] = zup_r[t, i]

        @pl.when(b < NG - 1)
        def _():
            arrived(zdn_r.at[t], f"h5{t}")
            for i in range(NT):
                cd[i, pl.ds(7, NG, stride=8), :] = zdn_r[t, i]

    def pigment_terms():
        sums = [jnp.zeros((32, 128), F32)] * 5
        rows = [jnp.zeros((8, 128), F32)] * 2
        for i in range(NT):
            p = pig_s[i]
            sums = [x + p * ref[i] for x, ref in zip(sums, (ce, cw, cd, cu, mix))]
            rows = [x + p * ref[0, i] for x, ref in zip(rows, (hn, hs))]
        for n, x in enumerate(sums):
            pst[n] = x
        for n, x in enumerate(rows):
            psn[n] = x

    def update(t):
        got, west, south = forcing(t)
        for r in range(NG):
            u, v, temp, d, dm, par = got[r]
            warm = jnp.exp(0.0633 * (temp - 20.0))
            uwest = jnp.where(lane8 == 0, west[r], roll(u, 1, 1))
            vsouth = got[r - 1][1] if r > 0 else south
            a_e = ops[0, r] * (jnp.maximum(u, 0.0) + 0.05)
            b_e = ops[0, r] * (0.05 - jnp.minimum(u, 0.0))
            a_w = ops[1, r] * (jnp.maximum(uwest, 0.0) + 0.05)
            b_w = ops[1, r] * (0.05 - jnp.minimum(uwest, 0.0))
            a_n = ops[2, r] * (jnp.maximum(v, 0.0) + 0.05)
            b_n = ops[2, r] * (0.05 - jnp.minimum(v, 0.0))
            a_s_ = ops[3, r] * (jnp.maximum(vsouth, 0.0) + 0.05)
            b_s = ops[3, r] * (0.05 - jnp.minimum(vsouth, 0.0))
            k0 = 1.0 - a_e - b_w - a_n - b_s - d - dm
            half = ops[4, r]
            warm = half * warm
            parw = half * par
            rows = pl.ds(8 * r, 8)
            if t == 0:
                new = k0 * ps[0, r] + (b_e * pst[0, rows, :] + a_w * pst[1, rows, :])
                new = new + (b_n * (ps[0, r + 1] if r < NG - 1 else psn[0]) + a_s_ * (ps[0, r - 1] if r > 0 else psn[1]))
                new = new + (d * pst[2, rows, :] + dm * pst[3, rows, :]) + warm * pst[4, rows, :]
                for i in range(NT):
                    photo = ph_s[i] * parw / (par + sat_s[i])
                    grown[i, rows, :] = photo
                    new = new + photo * (pig_s[i] * cs[t, i, rows, :])
                ps[1, r] = new
                for n, x in enumerate((k0, b_e, a_w, b_n, a_s_, d, dm, warm)):
                    kept[r, n] = x
            else:
                stencil(t, r, (k0, b_e, a_w, b_n, a_s_, d, dm, warm), lambda i: ph_s[i] * parw / (par + sat_s[i]))
        if t == 0:
            publish_light(1)
            for r in range(NG):
                stencil(t, r, [kept[r, n] for n in range(8)], lambda i: grown[i, pl.ds(8 * r, 8), :])

    def stencil(t, r, coefs, photo):
        k0, b_e, a_w, b_n, a_s_, d, dm, warm = coefs
        rows = pl.ds(8 * r, 8)

        def one(i, _):
            x = cs[t, i, rows, :]
            up = cs[t, i, pl.ds(8 * r + 8, 8), :] if r < NG - 1 else hn[t, i]
            dn = cs[t, i, pl.ds(8 * r - 8, 8), :] if r > 0 else hs[t, i]
            new = (
                (k0 + photo(i)) * x
                + (b_e * ce[i, rows, :] + a_w * cw[i, rows, :])
                + (b_n * up + a_s_ * dn)
                + (d * cd[i, rows, :] + dm * cu[i, rows, :])
                + warm * mix[i, rows, :]
            )
            if t == STEPS - 1:
                oc[pl.ds(i * 32 + r, 8, stride=4), :] = new
            else:
                cs[t + 1, i, rows, :] = new
            return 0

        lax.fori_loop(0, NT, one, 0, unroll=True)

    loads[3].wait()
    pig = [jnp.zeros((8, 128), F32)] * NG
    for n in range(3):
        loads[n].wait()
        for i in range(cuts[n], cuts[n + 1]):
            for r in range(NG):
                x = cin[pl.ds(i * 32 + r, 8, stride=4), :]
                cs[0, i, pl.ds(8 * r, 8), :] = x
                pig[r] = pig[r] + pig_s[i] * x
    for r in range(NG):
        ps[0, r] = pig[r]
    publish_light(0)
    publish_halos(0)
    for copy in loads[4:9] + [pltpu.make_async_copy(oc_in, oc_in, loc.at[7])]:
        copy.wait()
    share_fixed()
    local_terms(0)
    columns(0)
    share_state()
    openings()
    halos(0)
    pigment_terms()
    arrived(fqr.at[0:3], "fixed")
    arrived(fr.at[0:3], "force")
    arrived(dlr.at[0:3], "edge")
    arrived(ewr, "u", has_w)
    arrived(vsr, "v", has_s)
    update(0)
    publish_halos(1)
    local_terms(1)
    await_state()
    halos(1)
    await_light()
    update(1)

    sent()


def write_out(*refs):
    n = (len(refs) - 1) // 2
    copies = [pltpu.make_async_copy(refs[k], refs[n + k], refs[-1].at[k]) for k in range(n)]
    for copy in copies:
        copy.start()
    for copy in copies:
        copy.wait()


def per_device(nx, ny, *args):
    u, v, temp, sal, quiet, c, dep, sol, rates, photo, satur, pig = args
    shape = u.shape
    fields = [x.reshape(32, 128) for x in (u, v, temp, sal, quiet)]
    hbm = pl.BlockSpec(memory_space=pltpu.HBM)
    vmem = pl.BlockSpec(memory_space=pltpu.VMEM)
    col = jax.ShapeDtypeStruct((32, 128), F32)
    V = pltpu.VMEM
    D = pltpu.SemaphoreType.DMA
    S = STEPS
    out = pl.pallas_call(
        functools.partial(kernel, nx, ny),
        out_shape=(col, col, col, col, jax.ShapeDtypeStruct((NT * 32, 128), F32)),
        in_specs=[hbm] * 12,
        out_specs=(vmem,) * 5,
        scratch_shapes=[
            pltpu.SMEM((NT, NT), F32), pltpu.SMEM((NT,), F32), pltpu.SMEM((NT,), F32), pltpu.SMEM((NT,), F32),
            V((NT * 32, 128), F32), V((5, 32, 128), F32), V((4, 128), jnp.int32), V((4, 128), F32),
            V((S, NT, 32, 128), F32), V((S, NT, 8, 128), F32), V((S, NT, 8, 128), F32),
            V((S, NT, 4, 128), F32), V((S, NT, 4, 128), F32), V((S, NT, 4, 128), F32), V((S, NT, 4, 128), F32),
            V((S, 32, 128), F32), V((S, 32, 128), F32), V((S, 32, 128), F32), V((S, 32, 128), F32),
            V((S, NG, 8, 128), F32), V((S, 32, 128), F32),
            V((NG, NF, 8, 128), F32), V((NG, NF, 8, 128), F32),
            V((32, 128), F32), V((8, 128), F32),
            V((4, 4, 128), jnp.int32), V((5, NG, 8, 128), F32),
            V((NT, 32, 128), F32), V((NT, 32, 128), F32), V((NT, 32, 128), F32), V((NT, 32, 128), F32), V((NT, 32, 128), F32),
            V((5, 32, 128), F32), V((2, 8, 128), F32), V((NT, 32, 128), F32), V((NG, 8, 8, 128), F32),
            V((NG, 2, 8, 128), F32), V((NG, 1, 128), F32), V((NG, 1, 128), F32), V((2, 8, 128), F32), V((NG, 8, 128), F32),
            V((2, 2, 128), F32), V((NG, 2, 128), F32), V((2, 2, 128), F32), V((NG, 2, 128), F32),
            V((8, 128), F32), V((8, 128), F32), V((8, 128), F32),
            V((NG, 2, 8, 128), F32), V((NG, 2, 8, 128), F32), V((NG, 4, 8, 128), F32), V((NG, 4, 8, 128), F32),
            V((32, 128), F32), V((NG, 8, 128), F32), V((NG, 8, 128), F32), V((NG, 8, 128), F32),
            V((NG, 4, 8, 128), F32), V((4, 8, 128), F32), V((2, 4, 128), F32), V((6, 16, 128), F32),
            D((10,)), D((len(SEND),)), D((len(RECV),)),
        ],
        compiler_params=pltpu.CompilerParams(collective_id=0, has_side_effects=True, vmem_limit_bytes=16 << 20),
    )(*[pltpu.with_memory_space_constraint(x, pltpu.HBM) for x in (*fields, c.reshape(NT * 32, 128), dep, sol, rates, photo, satur, pig)])
    out = pl.pallas_call(
        write_out,
        out_shape=(col, col, col, col, jax.ShapeDtypeStruct((NT * 32, 128), F32)),
        in_specs=[vmem] * 5,
        out_specs=(hbm,) * 5,
        scratch_shapes=[D((5,))],
        compiler_params=pltpu.CompilerParams(vmem_limit_bytes=4 << 20),
    )(*out)
    return tuple(x.reshape(shape) for x in out[:4]) + (out[4].reshape(c.shape),)


def solution(mesh):
    field = P(None, "gy", "grp", "gx")
    tracer = P(None, "grp", "gy", "gx")
    flat = P("gy", "gx")
    return jax.shard_map(
        functools.partial(per_device, mesh.shape["gx"], mesh.shape["gy"]),
        mesh=mesh,
        in_specs=(field,) * 5 + (tracer, flat, flat, P(), P(), P(), P()),
        out_specs=(field,) * 4 + (tracer,),
        check_vma=False,
    )
```

```python
import functools

import jax
import jax.numpy as jnp
from jax import lax
from jax.experimental import pallas as pl
from jax.experimental.pallas import tpu as pltpu
from jax.sharding import PartitionSpec as P

STEPS = 2
NG = 4
NT = 19
F32 = jnp.float32
NF = 3
SEND = ("pig", "dep0", "dep1", "dep2", "dep3", "solw", "sols", "h0", "h1", "h2", "h3", "h4", "h5", "fixed", "force", "edge", "state", "v", "row", "u", "col", "sums", "ssum", "wsum", "span", "wpan", "cols")
RECV = SEND[:7] + tuple(f"h{n}{t}" for n in range(6) for t in range(2)) + SEND[13:]


def roll(x, shift, axis):
    return pltpu.roll(x, shift % x.shape[axis], axis)


def kernel(
    nx, ny,
    u_hbm, v_hbm, t_hbm, s_hbm, q_hbm, c_hbm, dep_hbm, sol_hbm, a_hbm, ph_hbm, sat_hbm, pig_hbm,
    ou, ov, ot, osl, oc,
    a_s, ph_s, sat_s, pig_s, cin, oc_in, dep, sol, cs, hs, hn, zup_s, zdn_s, zup_r, zdn_r, xe_s, xw_s, xe_r, xw_r,
    ps, pf, fs, fr, vsh, vsr, dpx, ops, mix, cw, ce, cu, cd,
    pst, psn, grown, kept, uv, dls, dlr, pcs, pcr, scs, scr, wcs, wcr, pws, pwr, psr, fs2, fr2, fqs, fqr, ep, ews, ewr, ewx, n2s, n2r, solx, wst,
    loc, ssems, rsems,
):
    b = lax.axis_index("grp")
    ix = lax.axis_index("gx")
    iy = lax.axis_index("gy")
    has_e, has_w, has_n, has_s = ix < nx - 1, ix > 0, iy < ny - 1, iy > 0
    east, west, north, south = {"gx": ix + 1}, {"gx": ix - 1}, {"gy": iy + 1}, {"gy": iy - 1}
    sides = ((has_w, west), (has_e, east), (has_s, south), (has_n, north))
    peers = [lax.rem(b + k, NG) for k in (2, 3, 1)]

    cuts = (0, 6, 13, NT)
    loads = []
    for n in range(3):
        part = pl.ds(32 * cuts[n], 32 * (cuts[n + 1] - cuts[n]))
        loads.append(pltpu.make_async_copy(c_hbm.at[part], cin.at[part], loc.at[(0, 8, 9)[n]]))
    for n, (ref, dst) in enumerate(((pig_hbm, pig_s), (dep_hbm, dep), (sol_hbm, sol), (a_hbm, a_s), (ph_hbm, ph_s), (sat_hbm, sat_s))):
        loads.append(pltpu.make_async_copy(ref, dst, loc.at[1 + n]))
    for n, ref in enumerate((u_hbm, v_hbm, t_hbm, s_hbm, q_hbm)):
        loads.append(pltpu.make_async_copy(ref, oc_in.at[n], loc.at[7]))
    for copy in loads:
        copy.start()

    barrier = pltpu.get_barrier_semaphore()
    for g in peers:
        pl.semaphore_signal(barrier, inc=1, device_id={"grp": g})
    for there, dev in sides[::-1]:

        @pl.when(there)
        def _():
            for g in range(NG):
                pl.semaphore_signal(barrier, inc=1, device_id={"grp": g, **dev})

    lane8 = lax.broadcasted_iota(jnp.int32, (8, 128), 1)
    lane32 = lax.broadcasted_iota(jnp.int32, (32, 128), 1)
    row8 = lax.broadcasted_iota(jnp.int32, (8, 128), 0)
    row16 = lax.broadcasted_iota(jnp.int32, (16, 128), 0)
    lane16 = lax.broadcasted_iota(jnp.int32, (16, 128), 1)
    row32 = lax.broadcasted_iota(jnp.int32, (32, 128), 0)
    pending = []

    def remote(src, dst, name, dev):
        tag, at = (name[:2], name) if name[0] == "h" else (name, name)
        return pltpu.make_async_remote_copy(src, dst, ssems.at[SEND.index(tag)], rsems.at[RECV.index(at)], device_id=dev, device_id_type=pl.DeviceIdType.MESH)

    def guarded(there, act):
        if there is None:
            act()
        else:
            pl.when(there)(act)

    def send(src, dst, name, dev, there=None, whole=None):
        if whole is not False:
            pending.append((there, src if whole is None else whole, name))
        guarded(there, remote(src, dst, name, dev).start)

    def sent(names=None):
        for there, ref, name in pending:
            if names is None or name in names:
                guarded(there, remote(ref, ref, name, {"grp": peers[0]}).wait_send)
        pending[:] = [x for x in pending if names is not None and x[2] not in names]

    def arrived(ref, name, there=None):
        guarded(there, remote(ref, ref, name, {"grp": peers[0]}).wait_recv)

    def first(k, ref):
        return ref if k == 0 else False

    for there, refs in ((has_w, (ewr, ewx, xw_r, pwr, wcr, solx.at[0])), (has_e, (xe_r,)), (has_s, (vsr, hs, n2r, psr, scr, solx.at[1])), (has_n, (hn,))):

        @pl.when(jnp.logical_not(there))
        def _():
            for ref in refs:
                ref[...] = jnp.zeros_like(ref)

    for k, (there, _) in enumerate(sides):

        @pl.when(jnp.logical_not(there))
        def _():
            dpx[k] = jnp.zeros((4, 128), jnp.int32)

    def publish_light(t):
        pf[t, pl.ds(pl.multiple_of(b * 8, 8), 8), :] = ps[t, b]
        mine = pf.at[t, pl.ds(pl.multiple_of(b * 8, 8), 8), :]
        if t == 0:
            pl.semaphore_wait(barrier, NG - 1 + NG * sum(there.astype(jnp.int32) for there, _ in sides))
            for k, g in enumerate(peers):
                send(ps.at[t, g], mine, "pig", {"grp": g}, whole=first(k, ps.at[t, 0:3]))
        else:
            def total(x):
                for n in (4, 2, 1):
                    x = x + roll(x, n, 0)
                return x[0:1]

            for r in range(NG):
                x = 0.01 + 0.05 * ps[t, r]
                whole = total(x)
                for n, edge in enumerate((x[7:8], x[0:1])):
                    pcs[n, r : r + 1] = whole
                    pcs[n, NG + r : NG + r + 1] = edge
            pack = jnp.zeros((8, 128), F32)
            for r in range(NG):
                pack = jnp.where(lane8 == r, roll(ps[t, r], r + 1, 1), pack)
            pws[...] = pack
            for ref, x in ((scs, ps[t, NG - 1]), (wcs, pack)):
                x = 0.01 + 0.05 * x
                whole = total(x)
                for n, edge in enumerate((x[7:8], x[0:1])):
                    ref[n, 0:1] = whole
                    ref[n, 1:2] = edge
            for k, g in enumerate(peers):
                send(pcs.at[(g < b).astype(jnp.int32)], pcr.at[b], "sums", {"grp": g}, whole=first(k, pcr.at[0:3]))
            for k, g in enumerate(peers):
                side = (g < b).astype(jnp.int32)
                send(scs.at[side], scr.at[b], "ssum", {"grp": g, **north}, has_n, first(k, scr.at[0:3]))
                send(wcs.at[side], wcr.at[b], "wsum", {"grp": g, **east}, has_e, first(k, wcr.at[0:3]))
            send(ps.at[t, NG - 1], psr, "span", north, has_n)
            send(pws, pwr, "wpan", east, has_e)
            pcr[b] = pcs[0]
            scr[b] = scs[0]
            wcr[b] = wcs[0]
        if t == 0:
            for k, (there, dev) in enumerate(sides):
                send(dep_hbm, dpx.at[k ^ 1], f"dep{k ^ 1}", dev, there)
            send(sol_hbm, solx.at[0], "solw", east, has_e)
            send(sol_hbm, solx.at[1], "sols", north, has_n)
    def publish_halos(t):
        mine = pf.at[t, pl.ds(pl.multiple_of(b * 8, 8), 8), :]
        if t == 1:
            for k, g in enumerate(peers):
                send(ps.at[t, g], mine, "cols", {"grp": g}, whole=first(k, ps.at[t, 0:3]))
            sent([f"h{n}0" for n in range(6)])
        send(cs.at[t, :, pl.ds(24, 8), :], hs.at[t], f"h0{t}", north, has_n)
        send(cs.at[t, :, pl.ds(0, 8), :], hn.at[t], f"h1{t}", south, has_s)
        pe = jnp.zeros((32, 128), F32)
        pw = jnp.zeros((32, 128), F32)
        for i in range(NT):
            x = cs[t, i]
            pe = jnp.where(lane32 == i, roll(x, i + 1, 1), pe)
            pw = jnp.where(lane32 == i, roll(x, i, 1) if i else x, pw)
        xe_s[t] = pe
        xw_s[t] = pw
        send(xe_s.at[t], xw_r.at[t], f"h2{t}", east, has_e)
        send(xw_s.at[t], xe_r.at[t], f"h3{t}", west, has_w)
        for i in range(NT):
            zup_s[t, i] = cs[t, i, pl.ds(7, NG, stride=8), :]
            zdn_s[t, i] = cs[t, i, pl.ds(0, NG, stride=8), :]

        send(zup_s.at[t], zup_r.at[t], f"h4{t}", {"grp": b + 1}, b < NG - 1)
        send(zdn_s.at[t], zdn_r.at[t], f"h5{t}", {"grp": b - 1}, b > 0)

    def local_terms(t):
        def mixing(i, _):
            acc = a_s[i, 0] * cs[t, 0]
            for j in range(1, NT):
                acc = acc + a_s[i, j] * cs[t, j]
            mix[i] = acc
            x = cs[t, i]
            cw[i] = roll(x, 1, 1)
            ce[i] = roll(x, 127, 1)
            cu[i] = roll(x, 1, 0)
            cd[i] = roll(x, 31, 0)
            return 0

        lax.fori_loop(0, NT, mixing, 0)

    def bound(x):
        return min(max(x, 0), 31)

    def edges(hi, lo):
        return jnp.where(row8 == 0, jnp.broadcast_to(hi, (8, 128)), jnp.broadcast_to(lo, (8, 128)))

    def share_fixed():
        for g in range(NG):
            hi, lo = bound(8 * g + 8), bound(8 * g - 1)
            for n, x in enumerate((0, 1, 4)):
                fqs[g, n] = oc_in[x, 8 * g : 8 * g + 8]
            for n, x in enumerate((0, 1, 4, 4)):
                fqs[g, 3, 2 * n : 2 * n + 1] = oc_in[x, hi : hi + 1]
                fqs[g, 3, 2 * n + 1 : 2 * n + 2] = oc_in[x, lo : lo + 1]
        for k, g in enumerate(peers):
            send(fqs.at[g], fqr.at[b], "fixed", {"grp": g}, whole=first(k, fqs.at[0:3]))
        fqr[b] = fqs[b]

    def columns(t):
        if t == 0:
            arrived(pf.at[t, 0:24], "pig")
            u, v, temp, sal = (oc_in[n] for n in range(4))
        else:
            u, v, temp, sal = ou[...], ov[...], ot[...], osl[...]
        att = 0.01 + 0.05 * pf[t]
        cum = att
        for s in (1, 2, 4, 8, 16):
            cum = cum + jnp.where(row32 >= s, roll(cum, s, 0), 0.0)
        top = sol[pl.ds(b, 1), :] * jnp.exp(att - cum)
        heating = top * (1.0 - jnp.exp(-att))
        wet = (row32 < dep[pl.ds(b, 1), :]).astype(F32)
        quiet = oc_in[4]
        temp = temp + 5.0 * heating * wet
        rho = 0.8 * sal - 0.2 * temp
        strat = roll(rho, 31, 0) - rho
        face = (0.5 * (quiet + roll(quiet, 31, 0)) + 0.15 * jax.nn.sigmoid(-strat)) * roll(wet, 31, 0)
        face = jnp.where(row32 < 31, face, 0.0)

        def stir(x):
            flux = face * (roll(x, 31, 0) - x)
            return x + flux - roll(flux, 1, 0)

        u, v, temp, sal = stir(u), stir(v), stir(temp), stir(sal)
        if t == 0:
            par = top * jnp.exp(-0.5 * att)
            for n, x in enumerate((temp, face, par)):
                for g in range(NG):
                    fs[g, n] = x[8 * g : 8 * g + 8]
            dls[0] = jnp.zeros((1, 128), F32)
            for g in range(1, NG):
                dls[g] = face[8 * g - 1 : 8 * g]
            vsh[...] = v
            for g in range(NG):
                send(vsh.at[pl.ds(8 * g, 8), :], vsr, "v", {"grp": g, **north}, jnp.logical_and(b == NG - 1, has_n), first(g, vsh))
            pack = jnp.zeros((32, 128), F32)
            for n, x in enumerate((u, temp, sal, quiet)):
                pack = jnp.where(lane32 == n, roll(x, n + 1, 1), pack)
            ep[...] = pack
            for g in range(NG):
                send(ep.at[8 * g : 8 * g + 8], ewr.at[b], "u", {"grp": g, **east}, has_e, first(g, ep))
            for k, g in enumerate(peers):
                send(fs.at[g], fr.at[b], "force", {"grp": g}, whole=first(k, fs.at[0:3]))
                send(dls.at[g], dlr.at[b], "edge", {"grp": g}, whole=first(k, dls.at[0:3]))
            fr[b] = fs[b]
            dlr[b] = dls[b]
        ou[...] = u
        ov[...] = v
        ot[...] = temp
        osl[...] = sal

    def share_state():
        for g in range(NG):
            hi, lo = bound(8 * g + 8), bound(8 * g - 1)
            fs2[g, 0] = osl[8 * g : 8 * g + 8]
            for n, x in enumerate((ou, ov, ot, osl)):
                fs2[g, 1, 2 * n : 2 * n + 1] = x[hi : hi + 1]
                fs2[g, 1, 2 * n + 1 : 2 * n + 2] = x[lo : lo + 1]
        for k, g in enumerate(peers):
            send(fs2.at[g], fr2.at[b], "state", {"grp": g}, whole=first(k, fs2.at[0:3]))
        fr2[b] = fs2[b]
        for g in range(NG):
            hi, lo = bound(8 * g + 8), bound(8 * g - 1)
            ews[g] = edges(ep[hi : hi + 1], ep[lo : lo + 1])
            send(ews.at[g], ewx.at[b], "col", {"grp": g, **east}, has_e, first(g, ews))
        quiet = oc_in.at[4]
        for g in range(NG):
            hi, lo = bound(8 * g + 8), bound(8 * g - 1)
            for n, x in enumerate((ot, osl, quiet)):
                n2s[g, n] = x[8 * g : 8 * g + 8]
            for n, x in enumerate((ov, ot, osl, quiet)):
                n2s[g, 3, 2 * n : 2 * n + 1] = x[hi : hi + 1]
                n2s[g, 3, 2 * n + 1 : 2 * n + 2] = x[lo : lo + 1]
            send(n2s.at[g], n2r, "row", {"grp": g, **north}, jnp.logical_and(b == NG - 1, has_n), first(g, n2s))

    def await_state():
        arrived(fr2.at[0:3], "state")
        arrived(ewx, "col", has_w)
        arrived(n2r, "row", has_s)
        arrived(solx.at[0], "solw", has_w)
        arrived(solx.at[1], "sols", has_s)
        for n in range(4):
            x = jnp.zeros((16, 128), F32)
            for r in range(NG):
                x = jnp.where(lane16 == r, roll(jnp.concatenate([ewr[r], ewx[r]], axis=0), r - n, 1), x)
            wst[n] = x
        for n, ref in ((4, dpx.at[0]), (5, solx.at[0])):
            x = jnp.zeros((16, 128), F32)
            for r in range(NG):
                row = jnp.broadcast_to(ref[r : r + 1, :].astype(F32), (16, 128))
                x = jnp.where(lane16 == r, roll(row, r + 1, 1), x)
            wst[n] = x

    def await_light():
        arrived(pcr.at[0:3], "sums")

    def await_sides():
        arrived(scr.at[0:3], "ssum", has_s)
        arrived(wcr.at[0:3], "wsum", has_w)
        arrived(psr, "span", has_s)
        arrived(pwr, "wpan", has_w)

    def window(state, edge, n):
        return jnp.concatenate([state, edges(edge[2 * n : 2 * n + 1, :], edge[2 * n + 1 : 2 * n + 2, :])], axis=0)

    level16 = (jnp.where(row16 <= 8, row16, -1) + 8 * b).astype(F32)
    has_above = jnp.logical_or(row16 <= 8, b > 0)

    below, over = jnp.minimum(b + 1, NG - 1), jnp.maximum(b - 1, 0)

    def band_ocean(pigment, total, edge, surface, depth, temp, sal, quiet, movers):
        prefix = jnp.zeros((1, 128), F32)
        for g in range(NG):
            prefix = prefix + jnp.where(g < b, total(g), 0.0)
        prefix = jnp.broadcast_to(prefix, (8, 128))
        own = 0.01 + 0.05 * pigment
        att_hi, att_lo = edge(below), edge(over)
        cum = own
        for s in (1, 2, 4):
            cum = cum + jnp.where(row8 >= s, roll(cum, s, 0), 0.0)
        att = jnp.concatenate([own, edges(att_hi, att_lo)], axis=0)
        above = jnp.concatenate([prefix + (cum - own), prefix + edges(cum[7:8], -att_lo)], axis=0)
        wet = jnp.where(level16 < depth, 1.0, 0.0)
        top = surface * jnp.exp(-above)
        temp = temp + 5.0 * (top * (1.0 - jnp.exp(-att))) * wet
        rho = 0.8 * sal - 0.2 * temp
        strat = roll(rho, 15, 0) - rho
        face = (0.5 * (quiet + roll(quiet, 15, 0)) + 0.15 * jax.nn.sigmoid(-strat)) * roll(wet, 15, 0)
        face = jnp.where(has_above, face, 0.0)

        def stir(x):
            flux = face * (roll(x, 15, 0) - x)
            return (x + flux - roll(flux, 1, 0))[0:8]

        par = top[0:8] * jnp.exp(-0.5 * own)
        return [stir(x) for x in movers] + [stir(temp), face[0:8], roll(face, 1, 0)[0:8], par]

    def forcing(t):
        got = []
        if t == 0:
            for r in range(NG):
                temp, d, par = (fr[r, n] for n in range(NF))
                dm = jnp.where(row8 == 0, jnp.broadcast_to(dlr[r], (8, 128)), roll(d, 1, 0))
                moved = []
                for n in range(2):
                    x = fqr[r, n]
                    hi = jnp.broadcast_to(fqr[r, 3, 2 * n : 2 * n + 1], (8, 128))
                    lo = jnp.broadcast_to(fqr[r, 3, 2 * n + 1 : 2 * n + 2], (8, 128))
                    x = x + d * (jnp.where(row8 == 7, hi, roll(x, 7, 0)) - x) - dm * (x - jnp.where(row8 == 0, lo, roll(x, 1, 0)))
                    uv[r, n] = x
                    moved.append(x)
                got.append(moved + [temp, d, dm, par])
            west = [ewr[r] for r in range(NG)]
            south = vsr[...]
        else:
            wide = lambda x: jnp.broadcast_to(x.astype(F32), (16, 128))
            for r in range(NG):
                u, v = (window(uv[r, n], fr2[r, 1], n) for n in range(2))
                temp = window(fr[r, 0], fr2[r, 1], 2)
                sal = window(fr2[r, 0], fr2[r, 1], 3)
                quiet = window(fqr[r, 2], fqr[r, 3], 2)
                got.append(band_ocean(ps[1, r], lambda g: pcr[g, r : r + 1], lambda g: pcr[g, NG + r : NG + r + 1], wide(sol[r : r + 1, :]), wide(dep[r : r + 1, :]), temp, sal, quiet, (u, v)))
            arrived(pf.at[1, 0:24], "cols")
            columns(1)
            await_sides()
            edge = n2r[3]
            v = window(vsr[...], edge, 0)
            temp, sal, quiet = (window(n2r[n], edge, n + 1) for n in range(3))
            south = band_ocean(psr[...], lambda g: scr[g, 0:1], lambda g: scr[g, 1:2], wide(solx[1, NG - 1 : NG, :]), wide(dpx[2, NG - 1 : NG, :]), temp, sal, quiet, (v,))[0]
            uw = band_ocean(pwr[...], lambda g: wcr[g, 0:1], lambda g: wcr[g, 1:2], wst[5], wst[4], wst[1], wst[2], wst[3], (wst[0],))[0]
            west = [roll(uw, -r, 1) if r else uw for r in range(NG)]
        return got, west, south

    def openings():
        for k in range(4):
            arrived(dpx.at[k], f"dep{k}", sides[k][0])
        level = (lax.broadcasted_iota(jnp.int32, (8, 128), 0) + 8 * b).astype(F32)

        def wet_of(rows):
            return jnp.where(level < jnp.broadcast_to(rows, (8, 128)), 1.0, 0.0)

        def row(ref, r):
            return jnp.broadcast_to(ref[r : r + 1, :].astype(F32), (8, 128))

        own = [row(dep, r) for r in range(NG)]
        wets = [wet_of(x) for x in own]
        wet_n = wet_of(row(dpx.at[3], 0))
        wet_s = wet_of(row(dpx.at[2], NG - 1))
        for r in range(NG):
            wet_e = jnp.where(lane8 == 127, roll(wet_of(row(dpx.at[1], r)), 127, 1), roll(wets[r], 127, 1))
            wet_w = jnp.where(lane8 == 0, roll(wet_of(row(dpx.at[0], r)), 1, 1), roll(wets[r], 1, 1))
            ops[0, r] = wets[r] * wet_e
            ops[1, r] = wets[r] * wet_w
            ops[2, r] = wets[r] * (wets[r + 1] if r < NG - 1 else wet_n)
            ops[3, r] = wets[r] * (wets[r - 1] if r > 0 else wet_s)
            ops[4, r] = 0.5 * wets[r]

    def halos(t):
        arrived(hs.at[t], f"h0{t}", has_s)
        arrived(hn.at[t], f"h1{t}", has_n)
        arrived(xw_r.at[t], f"h2{t}", has_w)
        arrived(xe_r.at[t], f"h3{t}", has_e)
        pw = xw_r[t]
        pe = xe_r[t]
        for i in range(NT):
            cw[i] = jnp.where(lane32 == 0, roll(pw, 128 - i, 1) if i else pw, cw[i])
            ce[i] = jnp.where(lane32 == 127, roll(pe, 127 - i, 1), ce[i])

        @pl.when(b > 0)
        def _():
            arrived(zup_r.at[t], f"h4{t}")
            for i in range(NT):
                cu[i, pl.ds(0, NG, stride=8), :] = zup_r[t, i]

        @pl.when(b < NG - 1)
        def _():
            arrived(zdn_r.at[t], f"h5{t}")
            for i in range(NT):
                cd[i, pl.ds(7, NG, stride=8), :] = zdn_r[t, i]

    def pigment_terms():
        sums = [jnp.zeros((32, 128), F32)] * 5
        rows = [jnp.zeros((8, 128), F32)] * 2
        for i in range(NT):
            p = pig_s[i]
            sums = [x + p * ref[i] for x, ref in zip(sums, (ce, cw, cd, cu, mix))]
            rows = [x + p * ref[0, i] for x, ref in zip(rows, (hn, hs))]
        for n, x in enumerate(sums):
            pst[n] = x
        for n, x in enumerate(rows):
            psn[n] = x

    def update(t):
        got, west, south = forcing(t)
        for r in range(NG):
            u, v, temp, d, dm, par = got[r]
            warm = jnp.exp(0.0633 * (temp - 20.0))
            uwest = jnp.where(lane8 == 0, west[r], roll(u, 1, 1))
            vsouth = got[r - 1][1] if r > 0 else south
            a_e = ops[0, r] * (jnp.maximum(u, 0.0) + 0.05)
            b_e = ops[0, r] * (0.05 - jnp.minimum(u, 0.0))
            a_w = ops[1, r] * (jnp.maximum(uwest, 0.0) + 0.05)
            b_w = ops[1, r] * (0.05 - jnp.minimum(uwest, 0.0))
            a_n = ops[2, r] * (jnp.maximum(v, 0.0) + 0.05)
            b_n = ops[2, r] * (0.05 - jnp.minimum(v, 0.0))
            a_s_ = ops[3, r] * (jnp.maximum(vsouth, 0.0) + 0.05)
            b_s = ops[3, r] * (0.05 - jnp.minimum(vsouth, 0.0))
            k0 = 1.0 - a_e - b_w - a_n - b_s - d - dm
            half = ops[4, r]
            warm = half * warm
            parw = half * par
            rows = pl.ds(8 * r, 8)
            if t == 0:
                new = k0 * ps[0, r] + (b_e * pst[0, rows, :] + a_w * pst[1, rows, :])
                new = new + (b_n * (ps[0, r + 1] if r < NG - 1 else psn[0]) + a_s_ * (ps[0, r - 1] if r > 0 else psn[1]))
                new = new + (d * pst[2, rows, :] + dm * pst[3, rows, :]) + warm * pst[4, rows, :]
                for i in range(NT):
                    photo = ph_s[i] * parw / (par + sat_s[i])
                    grown[i, rows, :] = photo
                    new = new + photo * (pig_s[i] * cs[t, i, rows, :])
                ps[1, r] = new
                for n, x in enumerate((k0, b_e, a_w, b_n, a_s_, d, dm, warm)):
                    kept[r, n] = x
            else:
                stencil(t, r, (k0, b_e, a_w, b_n, a_s_, d, dm, warm), lambda i: ph_s[i] * parw / (par + sat_s[i]))
        if t == 0:
            publish_light(1)
            for r in range(NG):
                stencil(t, r, [kept[r, n] for n in range(8)], lambda i: grown[i, pl.ds(8 * r, 8), :])

    def stencil(t, r, coefs, photo):
        k0, b_e, a_w, b_n, a_s_, d, dm, warm = coefs
        rows = pl.ds(8 * r, 8)

        def one(i, _):
            x = cs[t, i, rows, :]
            up = cs[t, i, pl.ds(8 * r + 8, 8), :] if r < NG - 1 else hn[t, i]
            dn = cs[t, i, pl.ds(8 * r - 8, 8), :] if r > 0 else hs[t, i]
            new = (
                (k0 + photo(i)) * x
                + (b_e * ce[i, rows, :] + a_w * cw[i, rows, :])
                + (b_n * up + a_s_ * dn)
                + (d * cd[i, rows, :] + dm * cu[i, rows, :])
                + warm * mix[i, rows, :]
            )
            if t == STEPS - 1:
                oc[pl.ds(i * 32 + r, 8, stride=4), :] = new
            else:
                cs[t + 1, i, rows, :] = new
            return 0

        lax.fori_loop(0, NT, one, 0, unroll=True)

    loads[3].wait()
    pig = [jnp.zeros((8, 128), F32)] * NG
    for n in range(3):
        loads[n].wait()
        for i in range(cuts[n], cuts[n + 1]):
            for r in range(NG):
                x = cin[pl.ds(i * 32 + r, 8, stride=4), :]
                cs[0, i, pl.ds(8 * r, 8), :] = x
                pig[r] = pig[r] + pig_s[i] * x
    for r in range(NG):
        ps[0, r] = pig[r]
    publish_light(0)
    publish_halos(0)
    for copy in loads[4:9] + [pltpu.make_async_copy(oc_in, oc_in, loc.at[7])]:
        copy.wait()
    share_fixed()
    local_terms(0)
    columns(0)
    share_state()
    openings()
    halos(0)
    pigment_terms()
    arrived(fqr.at[0:3], "fixed")
    arrived(fr.at[0:3], "force")
    arrived(dlr.at[0:3], "edge")
    arrived(ewr, "u", has_w)
    arrived(vsr, "v", has_s)
    update(0)
    publish_halos(1)
    local_terms(1)
    await_state()
    halos(1)
    await_light()
    update(1)

    sent()


def write_out(*refs):
    n = (len(refs) - 1) // 2
    copies = [pltpu.make_async_copy(refs[k], refs[n + k], refs[-1].at[k]) for k in range(n)]
    for copy in copies:
        copy.start()
    for copy in copies:
        copy.wait()


def per_device(nx, ny, *args):
    u, v, temp, sal, quiet, c, dep, sol, rates, photo, satur, pig = args
    shape = u.shape
    fields = [x.reshape(32, 128) for x in (u, v, temp, sal, quiet)]
    hbm = pl.BlockSpec(memory_space=pltpu.HBM)
    vmem = pl.BlockSpec(memory_space=pltpu.VMEM)
    col = jax.ShapeDtypeStruct((32, 128), F32)
    V = pltpu.VMEM
    D = pltpu.SemaphoreType.DMA
    S = STEPS
    out = pl.pallas_call(
        functools.partial(kernel, nx, ny),
        out_shape=(col, col, col, col, jax.ShapeDtypeStruct((NT * 32, 128), F32)),
        in_specs=[hbm] * 12,
        out_specs=(vmem,) * 5,
        scratch_shapes=[
            pltpu.SMEM((NT, NT), F32), pltpu.SMEM((NT,), F32), pltpu.SMEM((NT,), F32), pltpu.SMEM((NT,), F32),
            V((NT * 32, 128), F32), V((5, 32, 128), F32), V((4, 128), jnp.int32), V((4, 128), F32),
            V((S, NT, 32, 128), F32), V((S, NT, 8, 128), F32), V((S, NT, 8, 128), F32),
            V((S, NT, 4, 128), F32), V((S, NT, 4, 128), F32), V((S, NT, 4, 128), F32), V((S, NT, 4, 128), F32),
            V((S, 32, 128), F32), V((S, 32, 128), F32), V((S, 32, 128), F32), V((S, 32, 128), F32),
            V((S, NG, 8, 128), F32), V((S, 32, 128), F32),
            V((NG, NF, 8, 128), F32), V((NG, NF, 8, 128), F32),
            V((32, 128), F32), V((8, 128), F32),
            V((4, 4, 128), jnp.int32), V((5, NG, 8, 128), F32),
            V((NT, 32, 128), F32), V((NT, 32, 128), F32), V((NT, 32, 128), F32), V((NT, 32, 128), F32), V((NT, 32, 128), F32),
            V((5, 32, 128), F32), V((2, 8, 128), F32), V((NT, 32, 128), F32), V((NG, 8, 8, 128), F32),
            V((NG, 2, 8, 128), F32), V((NG, 1, 128), F32), V((NG, 1, 128), F32), V((2, 8, 128), F32), V((NG, 8, 128), F32),
            V((2, 2, 128), F32), V((NG, 2, 128), F32), V((2, 2, 128), F32), V((NG, 2, 128), F32),
            V((8, 128), F32), V((8, 128), F32), V((8, 128), F32),
            V((NG, 2, 8, 128), F32), V((NG, 2, 8, 128), F32), V((NG, 4, 8, 128), F32), V((NG, 4, 8, 128), F32),
            V((32, 128), F32), V((NG, 8, 128), F32), V((NG, 8, 128), F32), V((NG, 8, 128), F32),
            V((NG, 4, 8, 128), F32), V((4, 8, 128), F32), V((2, 4, 128), F32), V((6, 16, 128), F32),
            D((10,)), D((len(SEND),)), D((len(RECV),)),
        ],
        compiler_params=pltpu.CompilerParams(collective_id=0, has_side_effects=True, vmem_limit_bytes=16 << 20),
    )(*[pltpu.with_memory_space_constraint(x, pltpu.HBM) for x in (*fields, c.reshape(NT * 32, 128), dep, sol, rates, photo, satur, pig)])
    out = pl.pallas_call(
        write_out,
        out_shape=(col, col, col, col, jax.ShapeDtypeStruct((NT * 32, 128), F32)),
        in_specs=[vmem] * 5,
        out_specs=(hbm,) * 5,
        scratch_shapes=[D((5,))],
        compiler_params=pltpu.CompilerParams(vmem_limit_bytes=4 << 20),
    )(*out)
    return tuple(x.reshape(shape) for x in out[:4]) + (out[4].reshape(c.shape),)


def solution(mesh):
    field = P(None, "gy", "grp", "gx")
    tracer = P(None, "grp", "gy", "gx")
    flat = P("gy", "gx")
    return jax.shard_map(
        functools.partial(per_device, mesh.shape["gx"], mesh.shape["gy"]),
        mesh=mesh,
        in_specs=(field,) * 5 + (tracer, flat, flat, P(), P(), P(), P()),
        out_specs=(field,) * 4 + (tracer,),
        check_vma=False,
    )
```
